32 devices in a mesh: fsdp: 8 (over z, y), ctx: 4 (over x, core).
Axes of the slice: x: 2, y: 2, z: 4, core: 2. Of those that a mesh axis runs over, the one named last changes fastest.
Arguments:
- tokens: bfloat16 [2, 8, 512, 512], P(None, 'fsdp', 'ctx'), may hold values from -6 to 6
- lengths: int32 [2, 8], P(None, 'fsdp'), may hold values from 8 to 512, as said below
- cotangent: bfloat16 [2, 8, 512, 512], P(None, 'fsdp', 'ctx'), may hold values from -6 to 6
- first_up: bfloat16 [512, 2048], P('fsdp'), may hold values from -0.25 to 0.25
- first_down: bfloat16 [2048, 512], P('fsdp'), may hold values from -0.125 to 0.125
- project_in: bfloat16 [512, 1536], P('fsdp'), may hold values from -0.25 to 0.25
- project_out: bfloat16 [512, 512], P('fsdp'), may hold values from -1 to 1
- pointwise_in: bfloat16 [512, 1024], P('fsdp'), may hold values from -0.25 to 0.25
- depthwise: bfloat16 [512, 31], P('fsdp'), may hold values from -1 to 1
- pointwise_out: bfloat16 [512, 512], P('fsdp'), may hold values from -0.25 to 0.25
- second_up: bfloat16 [512, 2048], P('fsdp'), may hold values from -0.25 to 0.25
- second_down: bfloat16 [2048, 512], P('fsdp'), may hold values from -0.125 to 0.125
- gains: bfloat16 [6, 512], P(None, 'fsdp'), may hold values from 0.25 to 1.75
- batch_shift: bfloat16 [512], P('fsdp'), may hold values from -3 to 3
- head_terms: float32 [2, 8], replicated, may hold values from -3 to 300, as said below
Outputs:
- output: bfloat16 [2, 8, 512, 512], P(None, 'fsdp', 'ctx')
- grad_tokens: bfloat16 [2, 8, 512, 512], P(None, 'fsdp', 'ctx')
- grad_first_up: float32 [512, 2048], P('fsdp')
- grad_first_down: float32 [2048, 512], P('fsdp')
- grad_project_in: float32 [512, 1536], P('fsdp')
- grad_project_out: float32 [512, 512], P('fsdp')
- grad_pointwise_in: float32 [512, 1024], P('fsdp')
- grad_depthwise: float32 [512, 31], P('fsdp')
- grad_pointwise_out: float32 [512, 512], P('fsdp')
- grad_second_up: float32 [512, 2048], P('fsdp')
- grad_second_down: float32 [2048, 512], P('fsdp')
- grad_gains: float32 [6, 512], P(None, 'fsdp')
- grad_batch_shift: float32 [512], P('fsdp')
- grad_head_terms: float32 [2, 8], replicated
The draws below stay inside these ranges and needn't reach their ends.
Inputs may be any that keep to these rules, and one draw needn't show every extreme that they name: `lengths`: the first sequence of every micro-batch has all 512 frames. `head_terms`: row 0 is positive.
All inputs are finite; a program needn't handle non-finite values.
Results may differ from the reference program's by a relative error of at most 0.02.
Values may be sent and summed in bfloat16 or wider, within the bound.
A program may use at most 128 MiB of HBM per device.

```python
import math
import jax
import jax.numpy as jnp
from jax import lax

D = 512
H = 8
FF = 2048
KW = 31
HD = 64
LMAX = 512
RFAR = 256
MB = 2
NSEQ = 8


def draw_lengths(key, part):
    values = jax.random.randint(key, (MB, NSEQ), 8, LMAX + 1)
    return values.at[:, 0].set(LMAX).astype(jnp.int32)


def draw_head_terms(key, part):
    slope_key, far_key = jax.random.split(jax.random.fold_in(key, 17))
    slopes = jnp.exp(jax.random.uniform(slope_key, (H,), jnp.float32, math.log(0.002), math.log(0.15)))
    far = jax.random.uniform(far_key, (H,), jnp.float32, -3.0, 3.0)
    return jnp.stack([slopes, far]).astype(jnp.float32)


def level_of(key, shape, cuts, low, top_value):
    factor_of, own = 1.0, jax.random.fold_in(key, 6)
    for dim, blocks in cuts:
        heights = jnp.exp(jax.random.uniform(jax.random.fold_in(own, dim), (blocks,), jnp.float32, low / len(cuts), top_value / len(cuts)))
        factor_of = factor_of * jnp.repeat(heights, shape[dim] // blocks).reshape([-1 if axis == dim else 1 for axis in range(len(shape))])
    return factor_of


def bell_draw(own_key, dims, scale, limit, pieces=(), kind=jnp.bfloat16):
    loudness = level_of(own_key, dims, pieces, -0.22, 0.18) if pieces else 1.0
    array = jax.random.normal(own_key, dims, jnp.float32) * scale * loudness
    return jnp.minimum(jnp.maximum(array, -limit), limit).astype(kind)


def setup_inputs(seed: int = 0) -> dict:
    streams_of = jax.random.split(jax.random.key(seed), 16)
    return {
        "tokens": bell_draw(streams_of[0], (MB, NSEQ, LMAX, D), 1.0, 6.0, ((1, 8), (2, 4))),
        "lengths": draw_lengths(jax.random.fold_in(streams_of[15], 71), 0),
        "cotangent": bell_draw(streams_of[2], (MB, NSEQ, LMAX, D), 1.0, 6.0, ((1, 8), (2, 4))),
        "first_up": bell_draw(streams_of[3], (D, FF), D ** -0.5, 0.25, ((0, 8),)),
        "first_down": bell_draw(streams_of[4], (FF, D), FF ** -0.5, 0.125, ((0, 8),)),
        "project_in": bell_draw(streams_of[5], (D, 3 * D), D ** -0.5, 0.25, ((0, 8),)),
        "project_out": bell_draw(streams_of[6], (D, D), (D // 16) ** -0.5, 1.0, ((0, 8),)),
        "pointwise_in": bell_draw(streams_of[7], (D, 2 * D), D ** -0.5, 0.25, ((0, 8),)),
        "depthwise": bell_draw(streams_of[8], (D, KW), KW ** -0.5, 1.0, ((0, 8),)),
        "pointwise_out": bell_draw(streams_of[9], (D, D), D ** -0.5, 0.25, ((0, 8),)),
        "second_up": bell_draw(streams_of[10], (D, FF), D ** -0.5, 0.25, ((0, 8),)),
        "second_down": bell_draw(streams_of[11], (FF, D), FF ** -0.5, 0.125, ((0, 8),)),
        "gains": jnp.clip(1.0 + 0.15 * jax.random.normal(streams_of[12], (6, D), jnp.float32), 0.25, 1.75).astype(jnp.bfloat16),
        "batch_shift": bell_draw(streams_of[13], (D,), 0.5, 3.0, ((0, 8),)),
        "head_terms": draw_head_terms(jax.random.fold_in(streams_of[15], 71), 0),
    }


EPS = 1e-05
NEGATIVE = -1e+30

def product(left, right):
    return jnp.dot(left, right, preferred_element_type=jnp.float32)

def product_left(left, right):
    return jnp.dot(left.T, right, preferred_element_type=jnp.float32)

def product_right(left, right):
    return jnp.dot(left, right.T, preferred_element_type=jnp.float32)

def swish(value):
    return value * jax.nn.sigmoid(value)

def swish_slope(value):
    sigma = jax.nn.sigmoid(value)
    return sigma * (1.0 + value * (1.0 - sigma))

def layer_norm(stream, gain):
    centred = stream - lax.optimization_barrier(jnp.mean(stream, axis=-1, keepdims=True))
    inverse = lax.rsqrt(lax.optimization_barrier(jnp.mean(centred * centred, axis=-1, keepdims=True)) + EPS)
    unit = centred * inverse
    return ((unit * gain).astype(jnp.bfloat16), unit, inverse)

def norm_back(dnormed, unit, inverse, gain):
    scaled = dnormed * gain
    dstream = inverse * (scaled - lax.optimization_barrier(jnp.mean(scaled, axis=-1, keepdims=True)) - unit * lax.optimization_barrier(jnp.mean(scaled * unit, axis=-1, keepdims=True)))
    return (dstream, lax.optimization_barrier(jnp.sum(dnormed * unit, axis=0)))

def position_terms(query_start, rows, keys, head_terms):
    query_pos = query_start + lax.iota(jnp.int32, rows)
    key_pos = lax.iota(jnp.int32, keys)
    offset = query_pos[:, None] - key_pos[None, :]
    distance = jnp.abs(offset).astype(jnp.float32)
    far = (offset >= RFAR).astype(jnp.float32)
    bias = far[None] * head_terms[1][:, None, None] - distance[None] * head_terms[0][:, None, None]
    return (bias, distance, far)

def split_heads(queries, keyvals):
    rows, width = queries.shape
    keys = keyvals.shape[0]
    query_heads = queries.reshape(rows, H, HD).astype(jnp.float32)
    key_heads = keyvals[:, :width].reshape(keys, H, HD).astype(jnp.float32)
    value_heads = keyvals[:, width:].reshape(keys, H, HD).astype(jnp.float32)
    return (query_heads, key_heads, value_heads)

def score_heads(query_heads, key_heads, bias, key_valid):
    scores = jnp.einsum('qhd,khd->hqk', query_heads, key_heads)
    scores = scores * HD ** (-0.5) + bias
    return jnp.where(key_valid[None, None, :], scores, NEGATIVE)

def attend_forward(queries, keyvals, bias, key_valid):
    rows, width = queries.shape
    query_heads, key_heads, value_heads = split_heads(queries, keyvals)
    scores = score_heads(query_heads, key_heads, bias, key_valid)
    top = lax.optimization_barrier(jnp.max(scores, axis=-1, keepdims=True))
    logsum = top + jnp.log(lax.optimization_barrier(jnp.sum(jnp.exp(scores - top), axis=-1, keepdims=True)))
    probs = jnp.exp(scores - logsum).astype(jnp.bfloat16)
    context = jnp.einsum('hqk,khd->qhd', probs.astype(jnp.float32), value_heads)
    return (context.reshape(rows, width).astype(jnp.bfloat16), logsum)

def attend_backward(queries, keyvals, bias, distance, far, key_valid, logsum, dcontext):
    rows, width = queries.shape
    keys = keyvals.shape[0]
    query_heads, key_heads, value_heads = split_heads(queries, keyvals)
    scores = score_heads(query_heads, key_heads, bias, key_valid)
    probs = jnp.exp(scores - logsum)
    dcontext_heads = dcontext.reshape(rows, H, HD).astype(jnp.float32)
    dprobs = jnp.einsum('qhd,khd->hqk', dcontext_heads, value_heads)
    dscores = probs * (dprobs - lax.optimization_barrier(jnp.sum(probs * dprobs, axis=-1, keepdims=True)))
    slope_grad = -lax.optimization_barrier(jnp.sum(dscores * distance[None], axis=(1, 2)))
    far_grad = lax.optimization_barrier(jnp.sum(dscores * far[None], axis=(1, 2)))
    dscores_low = dscores.astype(jnp.bfloat16).astype(jnp.float32)
    probs_low = probs.astype(jnp.bfloat16).astype(jnp.float32)
    factor = HD ** (-0.5)
    dquery = jnp.einsum('hqk,khd->qhd', dscores_low, key_heads) * factor
    dkey = jnp.einsum('hqk,qhd->khd', dscores_low, query_heads) * factor
    dvalue = jnp.einsum('hqk,qhd->khd', probs_low, dcontext_heads)
    dkeyvals = jnp.concatenate([dkey.reshape(keys, width), dvalue.reshape(keys, width)], axis=1)
    return (dquery.reshape(rows, width), dkeyvals, jnp.stack([slope_grad, far_grad]))

def depthwise_apply(padded, kernel, count):
    kernel_f = kernel.astype(jnp.float32)
    padded_f = padded.astype(jnp.float32)
    total = jnp.zeros(padded.shape[:-2] + (count, padded.shape[-1]), jnp.float32)
    for tap in range(kernel.shape[1]):
        total = total + padded_f[..., tap:tap + count, :] * kernel_f[:, tap]
    return total

def depthwise_back(padded, dpadded, ddepth, kernel, count):
    kernel_f = kernel.astype(jnp.float32)
    padded_f = padded.astype(jnp.float32)
    span = kernel.shape[1] - 1
    dgated = jnp.zeros(ddepth.shape, jnp.float32)
    columns = []
    for tap in range(kernel.shape[1]):
        dgated = dgated + dpadded[..., span - tap:span - tap + count, :] * kernel_f[:, tap]
        columns.append(lax.optimization_barrier(jnp.sum((padded_f[..., tap:tap + count, :] * ddepth).reshape(-1, kernel.shape[0]), axis=0)))
    return (dgated, jnp.stack(columns, axis=1))

def front_pass(x_seq, length, weights, bias, half):
    first_up, first_down, project_in, project_out, pointwise_in, depthwise, pointwise_out, second_up, second_down, gains, batch_shift = weights
    gain_rows = gains.astype(jnp.float32)
    frames, width = x_seq.shape
    valid = lax.iota(jnp.int32, frames) < length
    mask = valid.astype(jnp.float32)[:, None]
    stream_in = x_seq.astype(jnp.float32)
    normed_first, unit_first, inverse_first = layer_norm(stream_in, gain_rows[0])
    up_first = product(normed_first, first_up)
    act_first = swish(up_first).astype(jnp.bfloat16)
    stream_first = stream_in + 0.5 * product(act_first, first_down)
    normed_attend, unit_attend, inverse_attend = layer_norm(stream_first, gain_rows[1])
    triple = product(normed_attend, project_in).astype(jnp.bfloat16)
    context, logsum = attend_forward(triple[:, :width], triple[:, width:], bias, valid)
    stream_attend = stream_first + product(context, project_out)
    normed_conv, unit_conv, inverse_conv = layer_norm(stream_attend, gain_rows[2])
    expanded = product(normed_conv, pointwise_in)
    linear = expanded[:, :width]
    gate_sigma = jax.nn.sigmoid(expanded[:, width:])
    gated_low = (linear * gate_sigma * mask).astype(jnp.bfloat16)
    padded = jnp.pad(gated_low, ((half, half), (0, 0)))
    depth = depthwise_apply(padded, depthwise, frames)
    return {'valid': valid, 'mask': mask, 'stream_in': stream_in, 'normed_first': normed_first, 'unit_first': unit_first, 'inverse_first': inverse_first, 'up_first': up_first, 'act_first': act_first, 'normed_attend': normed_attend, 'unit_attend': unit_attend, 'inverse_attend': inverse_attend, 'triple': triple, 'context': context, 'logsum': logsum, 'stream_attend': stream_attend, 'normed_conv': normed_conv, 'unit_conv': unit_conv, 'inverse_conv': inverse_conv, 'linear': linear, 'gate_sigma': gate_sigma, 'padded': padded, 'depth': depth}

def reference(tokens, lengths, cotangent, first_up, first_down, project_in, project_out, pointwise_in, depthwise, pointwise_out, second_up, second_down, gains, batch_shift, head_terms):
    weights = (first_up, first_down, project_in, project_out, pointwise_in, depthwise, pointwise_out, second_up, second_down, gains, batch_shift)
    half = KW // 2
    frames = LMAX
    width = D
    bias, distance, far = position_terms(0, frames, frames, head_terms)
    positions = lax.iota(jnp.int32, frames)
    gain_rows = gains.astype(jnp.float32)
    shift_row = batch_shift.astype(jnp.float32)
    outputs = []
    dinputs = []
    totals = None
    for micro in range(MB):
        batch_tokens = tokens[micro]
        batch_lengths = lengths[micro]
        batch_cot = cotangent[micro]

        def first_scan(item):
            state = front_pass(item[0], item[1], weights, bias, half)
            return (state['depth'], state['stream_attend'])
        depths, streams = lax.map(first_scan, (batch_tokens, batch_lengths))
        masks = (positions[None, :] < batch_lengths[:, None]).astype(jnp.float32)[:, :, None]
        count = jnp.sum(masks)
        bn_mean = lax.optimization_barrier(jnp.sum(masks * depths, axis=(0, 1))) / count
        centred = depths - bn_mean
        inverse_bn = lax.rsqrt(lax.optimization_barrier(jnp.sum(masks * centred * centred, axis=(0, 1))) / count + EPS)
        units_bn = centred * inverse_bn

        def rear_step(carry, item):
            unit_bn, stream_attend, dout_low = item
            shifted = unit_bn * gain_rows[5] + shift_row
            act_conv = swish(shifted).astype(jnp.bfloat16)
            stream_conv = stream_attend + product(act_conv, pointwise_out)
            normed_second, unit_second, inverse_second = layer_norm(stream_conv, gain_rows[3])
            up_second = product(normed_second, second_up)
            act_second = swish(up_second).astype(jnp.bfloat16)
            stream_second = stream_conv + 0.5 * product(act_second, second_down)
            out_low, unit_out, inverse_out = layer_norm(stream_second, gain_rows[4])
            dsecond_stream, gain_out = norm_back(dout_low.astype(jnp.float32), unit_out, inverse_out, gain_rows[4])
            dsecond_low = (0.5 * dsecond_stream).astype(jnp.bfloat16)
            dup_second = (product_right(dsecond_low, second_down) * swish_slope(up_second)).astype(jnp.bfloat16)
            dtemp, gain_second = norm_back(product_right(dup_second, second_up), unit_second, inverse_second, gain_rows[3])
            dconv_stream = dsecond_stream + dtemp
            dconv_low = dconv_stream.astype(jnp.bfloat16)
            dshift = product_right(dconv_low, pointwise_out) * swish_slope(shifted)
            step = (product_left(normed_second, dup_second), product_left(act_second, dsecond_low), product_left(act_conv, dconv_low), gain_second, gain_out, lax.optimization_barrier(jnp.sum(dshift * unit_bn, axis=0)), lax.optimization_barrier(jnp.sum(dshift, axis=0)))
            return (tuple((old + new for old, new in zip(carry, step))), (out_low, dshift, dconv_stream))
        rear_init = (jnp.zeros((width, FF), jnp.float32), jnp.zeros((FF, width), jnp.float32), jnp.zeros((width, width), jnp.float32), jnp.zeros((width,), jnp.float32), jnp.zeros((width,), jnp.float32), jnp.zeros((width,), jnp.float32), jnp.zeros((width,), jnp.float32))
        rear_sums, (out_lows, dshifts, dconv_streams) = lax.scan(rear_step, rear_init, (units_bn, streams, batch_cot))
        sum_shift = lax.optimization_barrier(jnp.sum(dshifts, axis=(0, 1)))
        sum_cross = lax.optimization_barrier(jnp.sum(dshifts * units_bn, axis=(0, 1)))

        def lower_step(carry, item):
            x_seq, length, unit_bn, dshift, dconv_stream = item
            state = front_pass(x_seq, length, weights, bias, half)
            mask = state['mask']
            ddepth = inverse_bn * gain_rows[5] * (dshift - mask * sum_shift / count - mask * unit_bn * sum_cross / count)
            dpadded = jnp.pad(ddepth, ((half, half), (0, 0)))
            dgated, grad_depth = depthwise_back(state['padded'], dpadded, ddepth, depthwise, frames)
            dgated = dgated * mask
            gate_sigma = state['gate_sigma']
            dexpanded = jnp.concatenate([dgated * gate_sigma, dgated * state['linear'] * gate_sigma * (1.0 - gate_sigma)], axis=1).astype(jnp.bfloat16)
            dtemp, gain_conv = norm_back(product_right(dexpanded, pointwise_in), state['unit_conv'], state['inverse_conv'], gain_rows[2])
            dattend_stream = dconv_stream + dtemp
            dattend_low = dattend_stream.astype(jnp.bfloat16)
            dcontext = product_right(dattend_low, project_out).astype(jnp.bfloat16)
            triple = state['triple']
            dquery, dkeyvals, dheads = attend_backward(triple[:, :width], triple[:, width:], bias, distance, far, state['valid'], state['logsum'], dcontext)
            dtriple = jnp.concatenate([dquery, dkeyvals], axis=1).astype(jnp.bfloat16)
            dtemp, gain_attend = norm_back(product_right(dtriple, project_in), state['unit_attend'], state['inverse_attend'], gain_rows[1])
            dfirst_stream = dattend_stream + dtemp
            dfirst_low = (0.5 * dfirst_stream).astype(jnp.bfloat16)
            dup_first = (product_right(dfirst_low, first_down) * swish_slope(state['up_first'])).astype(jnp.bfloat16)
            dtemp, gain_first = norm_back(product_right(dup_first, first_up), state['unit_first'], state['inverse_first'], gain_rows[0])
            dinput = (dfirst_stream + dtemp).astype(jnp.bfloat16)
            step = (product_left(state['normed_first'], dup_first), product_left(state['act_first'], dfirst_low), product_left(state['normed_attend'], dtriple), product_left(state['context'], dattend_low), product_left(state['normed_conv'], dexpanded), grad_depth, gain_first, gain_attend, gain_conv, dheads)
            return (tuple((old + new for old, new in zip(carry, step))), dinput)
        lower_init = (jnp.zeros((width, FF), jnp.float32), jnp.zeros((FF, width), jnp.float32), jnp.zeros((width, 3 * width), jnp.float32), jnp.zeros((width, width), jnp.float32), jnp.zeros((width, 2 * width), jnp.float32), jnp.zeros((width, KW), jnp.float32), jnp.zeros((width,), jnp.float32), jnp.zeros((width,), jnp.float32), jnp.zeros((width,), jnp.float32), jnp.zeros((2, H), jnp.float32))
        lower_sums, dinput_seqs = lax.scan(lower_step, lower_init, (batch_tokens, batch_lengths, units_bn, dshifts, dconv_streams))
        outputs.append(out_lows)
        dinputs.append(dinput_seqs)
        gain_grads = jnp.stack([lower_sums[6], lower_sums[7], lower_sums[8], rear_sums[3], rear_sums[4], rear_sums[5]])
        step_grads = (lower_sums[0], lower_sums[1], lower_sums[2], lower_sums[3], lower_sums[4], lower_sums[5], rear_sums[2], rear_sums[0], rear_sums[1], gain_grads, rear_sums[6], lower_sums[9])
        totals = step_grads if totals is None else tuple((old + new for old, new in zip(totals, step_grads)))
    return (jnp.stack(outputs), jnp.stack(dinputs), totals[0], totals[1], totals[2], totals[3], totals[4], totals[5], totals[6], totals[7], totals[8], totals[9], totals[10], totals[11])
```

```python
import functools

import jax
import jax.numpy as jnp
from jax import lax
from jax.experimental import pallas as pl
from jax.experimental.pallas import tpu as pltpu
from jax.sharding import PartitionSpec as P

H = 8
HD = 64
RFAR = 256
HALO = 16
VMEM_LIMIT = 60 * 1024 * 1024


EPS = 1e-05
NEGATIVE = -1e30
MESH = pl.DeviceIdType.MESH
ANY = pl.BlockSpec(memory_space=pl.ANY)
VMEM = pl.BlockSpec(memory_space=pltpu.VMEM)
SMEM = pl.BlockSpec(memory_space=pltpu.SMEM)


def rotated(index, step, count):
    return lax.rem(index + step + count, count)


def other_of(index):
    return index + 1 - 2 * lax.rem(index, 2)


def greet(peers):
    barrier = pltpu.get_barrier_semaphore()
    for peer in peers:
        pl.semaphore_signal(barrier, inc=1, device_id=peer, device_id_type=MESH)
    pl.semaphore_wait(barrier, len(peers))


def send(src, dst, send_sem, recv_sem, to):
    return pltpu.make_async_remote_copy(
        src_ref=src,
        dst_ref=dst,
        send_sem=send_sem,
        recv_sem=recv_sem,
        device_id=to,
        device_id_type=MESH,
    )


def gather_kernel(count, size, axis, pair, *refs):
    ins, outs = refs[:count], refs[count : 2 * count]
    keep, zs, zr, ys, yr, cs, cr = refs[2 * count :]
    me = lax.axis_index(axis)
    highs = size // 2
    low, high = lax.rem(me, 2), lax.div(me, 2)
    partner = other_of(me)

    def part(ref, mine=True):
        if pair is None:
            return ref
        width = ref.shape[-1] // 2
        side = lax.rem(lax.axis_index(pair), 2)
        start = pl.multiple_of((side if mine else 1 - side) * width, width)
        return ref.at[:, pl.ds(start, width)]

    peers = [{axis: 2 * rotated(high, d, highs) + low} for d in range(1, highs)]
    peers.append({axis: partner})
    if pair is not None:
        pair_to = {pair: other_of(lax.axis_index(pair))}
        peers.append(pair_to)
    greet(peers)

    def origin(d):
        return 2 * rotated(high, -d, highs)

    def along(a, d, landed=False):
        place = origin(d) + low if landed else me
        return send(
            part(ins[a]),
            part(outs[a].at[place]),
            zs.at[a, d],
            zr.at[a, d],
            {axis: 2 * rotated(high, d, highs) + low},
        )

    def across_first(a, landed=False):
        place = partner if landed else me
        return send(part(ins[a]), part(outs[a].at[place]), ys.at[a, 0], yr.at[a, 0], {axis: partner})

    def across(a, d, landed=False):
        place = origin(d) + (1 - low if landed else low)
        return send(
            part(outs[a].at[origin(d) + low]),
            part(outs[a].at[place]),
            ys.at[a, d],
            yr.at[a, d],
            {axis: partner},
        )

    def hand(a, place, landed=False):
        return send(
            part(outs[a].at[place]),
            part(outs[a].at[place], not landed),
            cs.at[a, place],
            cr.at[a, place],
            pair_to,
        )

    def steps(first, last, body):
        def step(i, carry):
            body(i)
            return carry

        lax.fori_loop(first, last, step, 0)

    def local(a):
        return pltpu.make_async_copy(ins[a], outs[a].at[me], keep.at[a])

    for a in range(count):
        steps(1, highs, lambda d: along(a, d).start())
        across_first(a).start()
    for a in range(count):
        local(a).start()

    def second(a):
        across_first(a, True).wait_recv()
        if pair is not None:
            hand(a, partner).start()

        def one(d):
            across(a, d, True).wait_recv()
            if pair is not None:
                hand(a, origin(d) + 1 - low).start()

        steps(1, highs, one)

    for a in range(count):

        def one(d):
            along(a, d, True).wait_recv()
            across(a, d).start()
            if pair is not None:
                hand(a, origin(d) + low).start()

        steps(1, highs, one)
        if a > 0:
            second(a - 1)
    second(count - 1)
    for a in range(count):
        if pair is not None:
            steps(1, size, lambda i: hand(a, rotated(me, i, size), True).wait_recv())
            steps(1, size, lambda i: hand(a, rotated(me, i, size)).wait_send())
        steps(1, highs, lambda d: along(a, d).wait_send())
        across_first(a).wait_send()
        steps(1, highs, lambda d: across(a, d).wait_send())
        local(a).wait()


def gather(arrays, axis, pair, ident):
    count, size = len(arrays), lax.axis_size(axis)
    highs = size // 2
    dma = pltpu.SemaphoreType.DMA
    return pl.pallas_call(
        functools.partial(gather_kernel, count, size, axis, pair),
        out_shape=[jax.ShapeDtypeStruct((size,) + a.shape, a.dtype) for a in arrays],
        in_specs=[VMEM] * count,
        out_specs=[ANY] * count,
        scratch_shapes=[
            dma((count,)),
            dma((count, highs)),
            dma((count, highs)),
            dma((count, highs)),
            dma((count, highs)),
            dma((count, size)),
            dma((count, size)),
        ],
        compiler_params=pltpu.CompilerParams(
            collective_id=ident, has_side_effects=True, vmem_limit_bytes=VMEM_LIMIT
        ),
        name="gather_" + axis,
    )(*arrays)


def scatter_kernel(count, size, axis, pair, pair_size, *refs):
    ins, outs = refs[:count], refs[count : 2 * count]
    scratch = refs[2 * count :]
    if pair is None:
        halves = ins
        rest = scratch
    else:
        halves = scratch[:count]
        rest = scratch[count:]
    lows, highs_in = rest[:count], rest[count : 2 * count]
    rest = rest[2 * count :]
    if pair is not None:
        cross = rest[:count]
        rest = rest[count:]
        cs, cr, xs, xr, fs, fr = rest[:6]
        rest = rest[6:]
    ys, yr, zs, zr = rest
    me = lax.axis_index(axis)
    highs = size // 2
    low, high = lax.rem(me, 2), lax.div(me, 2)
    partner = {axis: other_of(me)}
    peers = [{axis: 2 * rotated(high, d, highs) + low} for d in range(1, highs)]
    peers.append(partner)
    if pair is not None:
        spot = lax.axis_index(pair)
        side, place = lax.rem(spot, 2), lax.div(spot, 2)
        places = pair_size // 2
        pair_to = {pair: other_of(spot)}
        peers.append(pair_to)
        for e in range(1, places):
            peers.append({pair: 2 * rotated(place, e, places) + side})
    greet(peers)

    def columns(a, mine):
        width = halves[a].shape[-1]
        return pl.ds(pl.multiple_of((side if mine else 1 - side) * width, width), width)

    def first(a):
        return send(ins[a].at[:, :, :, columns(a, False)], halves[a], cs.at[a], cr.at[a], pair_to)

    def across(a):
        return send(halves[a].at[:, 1 - low], lows[a], ys.at[a], yr.at[a], partner)

    def along(a, d):
        to = rotated(high, d, highs)
        return send(
            lows[a].at[to],
            highs_in[a].at[d - 1],
            zs.at[a, d - 1],
            zr.at[a, d - 1],
            {axis: 2 * to + low},
        )

    def over(a, e, landed=False):
        slot = rotated(place, -e, places) if landed else place
        return send(
            cross[a].at[place],
            cross[a].at[slot],
            xs.at[a, e - 1],
            xr.at[a, e - 1],
            {pair: 2 * rotated(place, e, places) + side},
        )

    def final(a, landed=False):
        return send(
            outs[a].at[:, columns(a, True)],
            outs[a].at[:, columns(a, not landed)],
            fs.at[a],
            fr.at[a],
            pair_to,
        )

    def steps(first_step, last, body):
        def step(i, carry):
            body(i)
            return carry

        lax.fori_loop(first_step, last, step, 0)

    def stage_first(a):
        first(a).wait_recv()

        def one(i):
            for j in range(2):
                own = ins[a][i, j, :, columns(a, True)].astype(jnp.float32)
                halves[a][i, j] = (own + halves[a][i, j].astype(jnp.float32)).astype(jnp.bfloat16)

        steps(0, highs, one)
        across(a).start()

    def stage_across(a):
        across(a).wait_recv()

        def one(i):
            own = halves[a][i, low].astype(jnp.float32)
            lows[a][i] = (own + lows[a][i].astype(jnp.float32)).astype(jnp.bfloat16)

        steps(0, highs, one)
        steps(1, highs, lambda d: along(a, d).start())

    def stage_along(a):
        steps(1, highs, lambda d: along(a, d).wait_recv())

        def added(d, total):
            return total + highs_in[a][d - 1].astype(jnp.float32)

        total = lax.fori_loop(1, highs, added, lows[a][high].astype(jnp.float32))
        if pair is None:
            outs[a][...] = total.astype(outs[a].dtype)
            return
        cross[a][place] = total.astype(jnp.bfloat16)
        for e in range(1, places):
            over(a, e).start()

    def stage_over(a):
        for e in range(1, places):
            over(a, e, True).wait_recv()
        total = cross[a][0].astype(jnp.float32)
        for i in range(1, places):
            total = total + cross[a][i].astype(jnp.float32)
        outs[a][:, columns(a, True)] = total
        final(a).start()

    if pair is None:
        stages = [stage_across, stage_along]
        for a in range(count):
            across(a).start()
    else:
        stages = [stage_first, stage_across, stage_along, stage_over]
        for a in range(count):
            first(a).start()
    for step in range(count + len(stages) - 1):
        for index, stage in enumerate(stages):
            if 0 <= step - index < count:
                stage(step - index)
    for a in range(count):
        across(a).wait_send()
        steps(1, highs, lambda d: along(a, d).wait_send())
        if pair is not None:
            first(a).wait_send()
            for e in range(1, places):
                over(a, e).wait_send()
            final(a, True).wait_recv()
            final(a).wait_send()


def scatter(arrays, axis, pair, dtype, ident):
    count, size = len(arrays), lax.axis_size(axis)
    highs = size // 2
    dma = pltpu.SemaphoreType.DMA
    low_type = jnp.bfloat16
    pair_size = 2 if pair is None else lax.axis_size(pair)
    split = 1 if pair is None else 2
    tail = [(a.shape[2], a.shape[3] // split) for a in arrays]
    scratch = []
    if pair is not None:
        scratch += [pltpu.VMEM((highs, 2) + t, low_type) for t in tail]
    scratch += [pltpu.VMEM((highs,) + t, low_type) for t in tail]
    scratch += [pltpu.VMEM((highs - 1,) + t, low_type) for t in tail]
    if pair is not None:
        scratch += [pltpu.VMEM((pair_size // 2,) + t, low_type) for t in tail]
        others = (count, pair_size // 2)
        scratch += [dma((count,)), dma((count,)), dma(others), dma(others)]
        scratch += [dma((count,)), dma((count,))]
    scratch += [dma((count,)), dma((count,)), dma((count, highs)), dma((count, highs))]
    return pl.pallas_call(
        functools.partial(scatter_kernel, count, size, axis, pair, pair_size),
        out_shape=[jax.ShapeDtypeStruct(a.shape[2:], dtype) for a in arrays],
        in_specs=[VMEM] * count,
        out_specs=[VMEM] * count,
        scratch_shapes=scratch,
        compiler_params=pltpu.CompilerParams(
            collective_id=ident, has_side_effects=True, vmem_limit_bytes=VMEM_LIMIT
        ),
        name="scatter_" + axis,
    )(*arrays)


def merge_sums(parts):
    total = parts[0]
    for part in parts[1:]:
        total = total + part
    return total


def merge_moments(micro, parts):
    total = merge_sums(parts)
    sums, squares, counts = (slice(i * micro, (i + 1) * micro) for i in range(3))
    mean = total[sums] / jnp.maximum(total[counts], 1.0)
    spread = total[squares]
    for part in parts:
        shift = part[sums] / jnp.maximum(part[counts], 1.0) - mean
        spread = spread + part[counts] * shift * shift
    return jnp.concatenate([total[sums], spread, total[counts], total[3 * micro :]], axis=0)


def channel_kernel(merge, sizes, axes, in_ref, out_ref, *refs):
    slots, sums = refs[:2], refs[2]
    sems = refs[3:]
    peers = []
    for axis, size in zip(axes, sizes):
        for d in range(1, size):
            peers.append({axis: rotated(lax.axis_index(axis), d, size)})
    greet(peers)
    source = in_ref
    for stage, (axis, size) in enumerate(zip(axes, sizes)):
        me = lax.axis_index(axis)
        slot, ss, rs = slots[stage], sems[2 * stage], sems[2 * stage + 1]

        def copy(d, landed=False):
            place = rotated(me, -d, size) if landed else me
            return send(
                source, slot.at[place], ss.at[d], rs.at[d], {axis: rotated(me, d, size)}
            )

        for d in range(1, size):
            copy(d).start()
        slot[me] = source[...]
        for d in range(1, size):
            copy(d, True).wait_recv()
        total = merge([slot[i] for i in range(size)])
        for d in range(1, size):
            copy(d).wait_send()
        target = sums if stage == 0 else out_ref
        target[...] = total
        source = sums


def channel_merge(rows, merge, ident):
    axes = ("ctx", "fsdp")
    sizes = tuple(lax.axis_size(axis) for axis in axes)
    dma = pltpu.SemaphoreType.DMA
    scratch = [pltpu.VMEM((size,) + rows.shape, rows.dtype) for size in sizes]
    scratch.append(pltpu.VMEM(rows.shape, rows.dtype))
    for size in sizes:
        scratch += [dma((size,)), dma((size,))]
    return pl.pallas_call(
        functools.partial(channel_kernel, merge, sizes, axes),
        out_shape=jax.ShapeDtypeStruct(rows.shape, rows.dtype),
        in_specs=[VMEM],
        out_specs=VMEM,
        scratch_shapes=scratch,
        compiler_params=pltpu.CompilerParams(collective_id=ident, has_side_effects=True),
        name="channel_merge_" + str(ident),
    )(rows)


def positions(start, rows, keys):
    query = start + lax.broadcasted_iota(jnp.int32, (rows, keys), 0)
    key = lax.broadcasted_iota(jnp.int32, (rows, keys), 1)
    offset = query - key
    distance = jnp.abs(offset).astype(jnp.float32)
    far = (offset >= RFAR).astype(jnp.float32)
    return distance, far, key


def head_probs(query, keys, terms_ref, head, distance, far, valid):
    scores = lax.dot_general(
        query, keys, (((1,), (1,)), ((), ())), preferred_element_type=jnp.float32
    )
    bias = far * terms_ref[1, head] - distance * terms_ref[0, head]
    scores = jnp.where(valid, scores * HD ** (-0.5) + bias, NEGATIVE)
    top = jnp.max(scores, axis=-1, keepdims=True)
    raised = jnp.exp(scores - top)
    return raised / jnp.sum(raised, axis=-1, keepdims=True)


def attend_kernel(start_ref, lengths_ref, terms_ref, q_ref, kv_ref, out_ref):
    rows, width = q_ref.shape[1:]
    keys = kv_ref.shape[0] * kv_ref.shape[2]
    distance, far, key = positions(start_ref[0], rows, keys)
    valid = key < lengths_ref[pl.program_id(0)]
    for head in range(H):
        cols = slice(head * HD, (head + 1) * HD)
        key_head = kv_ref[:, 0, :, cols].reshape(keys, HD)
        value_head = kv_ref[:, 0, :, width + head * HD : width + (head + 1) * HD].reshape(keys, HD)
        probs = head_probs(q_ref[0, :, cols], key_head, terms_ref, head, distance, far, valid)
        context = jnp.dot(
            probs.astype(jnp.bfloat16), value_head, preferred_element_type=jnp.float32
        )
        out_ref[0, :, cols] = context.astype(jnp.bfloat16)


def attend_back_kernel(
    start_ref, lengths_ref, terms_ref, q_ref, kv_ref, dctx_ref, dq_ref, dkv_ref, heads_ref
):
    rows, width = q_ref.shape[1:]
    shards, _, local, _ = kv_ref.shape
    keys = shards * local
    distance, far, key = positions(start_ref[0], rows, keys)
    valid = key < lengths_ref[pl.program_id(0)]
    factor = HD ** (-0.5)
    for head in range(H):
        cols = slice(head * HD, (head + 1) * HD)
        value_cols = slice(width + head * HD, width + (head + 1) * HD)
        query = q_ref[0, :, cols]
        key_head = kv_ref[:, 0, :, cols].reshape(keys, HD)
        value_head = kv_ref[:, 0, :, value_cols].reshape(keys, HD)
        dcontext = dctx_ref[0, :, cols]
        probs = head_probs(query, key_head, terms_ref, head, distance, far, valid)
        dprobs = lax.dot_general(
            dcontext, value_head, (((1,), (1,)), ((), ())), preferred_element_type=jnp.float32
        )
        dscores = probs * (dprobs - jnp.sum(probs * dprobs, axis=-1, keepdims=True))
        heads_ref[0, head : head + 1, :] = -jnp.sum(dscores * distance, axis=0, keepdims=True)
        heads_ref[0, H + head : H + head + 1, :] = jnp.sum(dscores * far, axis=0, keepdims=True)
        low = dscores.astype(jnp.bfloat16)
        dquery = jnp.dot(low, key_head, preferred_element_type=jnp.float32) * factor
        dq_ref[0, :, cols] = dquery.astype(jnp.bfloat16)
        dkey = (
            lax.dot_general(low, query, (((0,), (0,)), ((), ())), preferred_element_type=jnp.float32)
            * factor
        )
        dvalue = lax.dot_general(
            probs.astype(jnp.bfloat16),
            dcontext,
            (((0,), (0,)), ((), ())),
            preferred_element_type=jnp.float32,
        )
        dkv_ref[:, 0, :, cols] = dkey.astype(jnp.bfloat16).reshape(shards, local, HD)
        dkv_ref[:, 0, :, value_cols] = dvalue.astype(jnp.bfloat16).reshape(shards, local, HD)


def attend(start, lengths, terms, queries, keyvals):
    batch, rows, width = queries.shape
    shards, _, local, double = keyvals.shape
    block = pl.BlockSpec((1, rows, width), lambda b: (b, 0, 0))
    wide = pl.BlockSpec((shards, 1, local, double), lambda b: (0, b, 0, 0))
    return pl.pallas_call(
        attend_kernel,
        grid=(batch,),
        out_shape=jax.ShapeDtypeStruct(queries.shape, jnp.bfloat16),
        in_specs=[SMEM, SMEM, SMEM, block, wide],
        out_specs=block,
        compiler_params=pltpu.CompilerParams(vmem_limit_bytes=VMEM_LIMIT),
        name="attend",
    )(start, lengths, terms, queries, keyvals)


def attend_back(start, lengths, terms, queries, keyvals, dcontext):
    batch, rows, width = queries.shape
    shards, _, local, double = keyvals.shape
    keys = shards * local
    block = pl.BlockSpec((1, rows, width), lambda b: (b, 0, 0))
    wide = pl.BlockSpec((shards, 1, local, double), lambda b: (0, b, 0, 0))
    heads = pl.BlockSpec((1, 2 * H, keys), lambda b: (b, 0, 0))
    return pl.pallas_call(
        attend_back_kernel,
        grid=(batch,),
        out_shape=[
            jax.ShapeDtypeStruct(queries.shape, jnp.bfloat16),
            jax.ShapeDtypeStruct(keyvals.shape, jnp.bfloat16),
            jax.ShapeDtypeStruct((batch, 2 * H, keys), jnp.float32),
        ],
        in_specs=[SMEM, SMEM, SMEM, block, wide, block],
        out_specs=[block, wide, heads],
        compiler_params=pltpu.CompilerParams(vmem_limit_bytes=VMEM_LIMIT),
        name="attend_back",
    )(start, lengths, terms, queries, keyvals, dcontext)


def depth_kernel(taps, padded_ref, weight_ref, out_ref, wide):
    rows = out_ref.shape[1]
    wide[...] = padded_ref[0].astype(jnp.float32)
    shift = HALO - taps // 2
    total = wide[shift : shift + rows, :] * weight_ref[0:1, :]
    for tap in range(1, taps):
        total = total + wide[shift + tap : shift + tap + rows, :] * weight_ref[tap : tap + 1, :]
    out_ref[0] = total


def depth_back_kernel(
    taps, padded_ref, dlow_ref, dhigh_ref, ddepth_ref, weight_ref, dgated_ref, grad_ref, wide, dwide
):
    rows = ddepth_ref.shape[1]
    wide[...] = padded_ref[0].astype(jnp.float32)
    ddepth = ddepth_ref[0]
    dwide[0:HALO, :] = dlow_ref[0].astype(jnp.float32)
    dwide[HALO : HALO + rows, :] = ddepth
    dwide[HALO + rows :, :] = dhigh_ref[0].astype(jnp.float32)
    half = taps // 2
    total = jnp.zeros_like(ddepth)
    for tap in range(taps):
        at = HALO + half - tap
        total = total + dwide[at : at + rows, :] * weight_ref[tap : tap + 1, :]
        at = HALO - half + tap
        grad_ref[0, tap : tap + 1, :] = jnp.sum(
            wide[at : at + rows, :] * ddepth, axis=0, keepdims=True
        )
    grad_ref[0, taps:, :] = jnp.zeros_like(grad_ref[0, taps:, :])
    dgated_ref[0] = total


def lanes(rows, width):
    return pl.BlockSpec((1, rows, 128), lambda b, c: (b, 0, c))


def depth_apply(padded, weights, taps):
    batch, span, width = padded.shape
    rows = span - 2 * HALO
    weight = pl.BlockSpec((weights.shape[0], 128), lambda b, c: (0, c))
    return pl.pallas_call(
        functools.partial(depth_kernel, taps),
        grid=(batch, width // 128),
        out_shape=jax.ShapeDtypeStruct((batch, rows, width), jnp.float32),
        in_specs=[lanes(span, width), weight],
        out_specs=lanes(rows, width),
        scratch_shapes=[pltpu.VMEM((span, 128), jnp.float32)],
        name="depth_apply",
    )(padded, weights)


def depth_back(padded, dlow, dhigh, ddepth, weights, taps):
    batch, span, width = padded.shape
    rows = span - 2 * HALO
    padded_taps = weights.shape[0]
    weight = pl.BlockSpec((padded_taps, 128), lambda b, c: (0, c))
    return pl.pallas_call(
        functools.partial(depth_back_kernel, taps),
        grid=(batch, width // 128),
        out_shape=[
            jax.ShapeDtypeStruct((batch, rows, width), jnp.float32),
            jax.ShapeDtypeStruct((batch, padded_taps, width), jnp.float32),
        ],
        in_specs=[
            lanes(span, width),
            lanes(HALO, width),
            lanes(HALO, width),
            lanes(rows, width),
            weight,
        ],
        out_specs=[lanes(rows, width), lanes(padded_taps, width)],
        scratch_shapes=[
            pltpu.VMEM((span, 128), jnp.float32),
            pltpu.VMEM((span, 128), jnp.float32),
        ],
        name="depth_back",
    )(padded, dlow, dhigh, ddepth, weights)


def edges(block, width):
    count = lax.axis_size("ctx")
    forward = [(i, i + 1) for i in range(count - 1)]
    backward = [(target, source) for source, target in forward]
    low = lax.ppermute(block[:, block.shape[1] - width :], "ctx", forward)
    high = lax.ppermute(block[:, :width], "ctx", backward)
    return low, high


def product(left, right):
    return jnp.dot(left, right, preferred_element_type=jnp.float32)


def product_left(left, right):
    return jnp.dot(left.T, right, preferred_element_type=jnp.float32)


def product_right(left, right):
    return jnp.dot(left, right.T, preferred_element_type=jnp.float32)


def swish(value):
    return value * jax.nn.sigmoid(value)


def swish_slope(value):
    sigma = jax.nn.sigmoid(value)
    return sigma * (1.0 + value * (1.0 - sigma))


def layer_norm(stream, gain):
    centred = stream - jnp.mean(stream, axis=-1, keepdims=True)
    inverse = lax.rsqrt(jnp.mean(centred * centred, axis=-1, keepdims=True) + EPS)
    unit = centred * inverse
    return ((unit * gain).astype(jnp.bfloat16), unit, inverse)


def norm_back(dnormed, unit, inverse, gain):
    scaled = dnormed * gain
    dstream = inverse * (
        scaled
        - jnp.mean(scaled, axis=-1, keepdims=True)
        - unit * jnp.mean(scaled * unit, axis=-1, keepdims=True)
    )
    return (dstream, jnp.sum(dnormed * unit, axis=0))


def per_device(
    tokens,
    lengths,
    cotangent,
    first_up,
    first_down,
    project_in,
    project_out,
    pointwise_in,
    depthwise,
    pointwise_out,
    second_up,
    second_down,
    gains,
    batch_shift,
    head_terms,
):
    micro_count, seqs, local, width = tokens.shape
    batch = micro_count * seqs
    rows = batch * local
    shards = lax.axis_size("fsdp")
    taps = depthwise.shape[1]
    tap_rows = -(-taps // 8) * 8
    gain_count = gains.shape[0]
    bf16 = jnp.bfloat16
    start = (lax.axis_index("ctx") * local).astype(jnp.int32).reshape(1)
    frame_pos = start[0] + lax.iota(jnp.int32, local)
    lengths_flat = lengths.reshape(batch)
    mask = (frame_pos[None, :] < lengths_flat[:, None]).astype(jnp.float32).reshape(rows, 1)
    mask_micro = mask.reshape(micro_count, seqs * local, 1)

    whole_second_up = lax.all_gather(second_up, "fsdp", axis=0, tiled=True)
    whole_second_down = lax.all_gather(second_down, "fsdp", axis=0, tiled=True)
    small = jnp.concatenate([depthwise, gains.T, batch_shift[:, None]], axis=1)
    small_cols = small.shape[1]
    small_width = 256
    small = jnp.pad(small, ((0, 0), (0, small_width - small_cols)))
    gathered = gather(
        [first_up, small, first_down, project_in, project_out, pointwise_in, pointwise_out],
        "fsdp",
        "ctx",
        0,
    )
    gathered = [a.reshape(a.shape[0] * a.shape[1], a.shape[2]) for a in gathered]
    (
        whole_first_up,
        whole_small,
        whole_first_down,
        whole_project_in,
        whole_project_out,
        whole_pointwise_in,
        whole_pointwise_out,
    ) = gathered
    small_rows = whole_small[:, :small_cols].astype(jnp.float32).T
    tap_weights = jnp.pad(small_rows[:taps], ((0, tap_rows - taps), (0, 0)))
    gain_rows = small_rows[taps : taps + gain_count]
    shift_row = small_rows[taps + gain_count]

    stream_in = tokens.reshape(rows, width).astype(jnp.float32)
    normed_first, unit_first, inverse_first = layer_norm(stream_in, gain_rows[0])
    up_first = product(normed_first, whole_first_up)
    act_first = swish(up_first).astype(bf16)
    stream_first = stream_in + 0.5 * product(act_first, whole_first_down)
    normed_attend, unit_attend, inverse_attend = layer_norm(stream_first, gain_rows[1])
    triple = product(normed_attend, whole_project_in).astype(bf16)
    queries = triple[:, :width].reshape(batch, local, width)
    (keyvals,) = gather([triple[:, width:].reshape(batch, local, 2 * width)], "ctx", None, 1)
    context = attend(start, lengths_flat, head_terms, queries, keyvals).reshape(rows, width)
    stream_attend = stream_first + product(context, whole_project_out)
    normed_conv, unit_conv, inverse_conv = layer_norm(stream_attend, gain_rows[2])
    expanded = product(normed_conv, whole_pointwise_in)
    linear = expanded[:, :width]
    gate_sigma = jax.nn.sigmoid(expanded[:, width:])
    gated_low = (linear * gate_sigma * mask).astype(bf16).reshape(batch, local, width)
    low, high = edges(gated_low, HALO)
    padded = jnp.concatenate([low, gated_low, high], axis=1)
    depth = depth_apply(padded, tap_weights, taps).reshape(micro_count, seqs * local, width)

    own_count = jnp.sum(mask_micro, axis=1)
    own_sum = jnp.sum(mask_micro * depth, axis=1)
    own_mean = own_sum / jnp.maximum(own_count, 1.0)
    own_centred = depth - own_mean[:, None, :]
    own_spread = jnp.sum(mask_micro * own_centred * own_centred, axis=1)
    moments = jnp.concatenate(
        [own_sum, own_spread, jnp.broadcast_to(own_count, own_sum.shape)], axis=0
    )
    moment_rows = -(-moments.shape[0] // 8) * 8
    moments = jnp.pad(moments, ((0, moment_rows - moments.shape[0]), (0, 0)))
    moments = channel_merge(moments, functools.partial(merge_moments, micro_count), 2)
    count = moments[2 * micro_count : 3 * micro_count][:, None, :]
    bn_mean = moments[:micro_count][:, None, :] / count
    inverse_bn = lax.rsqrt(moments[micro_count : 2 * micro_count][:, None, :] / count + EPS)
    unit_bn = (depth - bn_mean) * inverse_bn
    shifted = unit_bn * gain_rows[5] + shift_row
    act_conv = swish(shifted).astype(bf16).reshape(rows, width)
    stream_conv = stream_attend + product(act_conv, whole_pointwise_out)
    normed_second, unit_second, inverse_second = layer_norm(stream_conv, gain_rows[3])
    up_second = product(normed_second, whole_second_up)
    act_second = swish(up_second).astype(bf16)
    stream_second = stream_conv + 0.5 * product(act_second, whole_second_down)
    out_low, unit_out, inverse_out = layer_norm(stream_second, gain_rows[4])
    output = out_low.reshape(tokens.shape)

    dout = cotangent.reshape(rows, width).astype(jnp.float32)
    dsecond_stream, gain_out = norm_back(dout, unit_out, inverse_out, gain_rows[4])
    dsecond_low = (0.5 * dsecond_stream).astype(bf16)
    dup_second = (product_right(dsecond_low, whole_second_down) * swish_slope(up_second)).astype(
        bf16
    )
    dtemp, gain_second = norm_back(
        product_right(dup_second, whole_second_up), unit_second, inverse_second, gain_rows[3]
    )
    grad_second_up = product_left(normed_second, dup_second)
    grad_second_down = product_left(act_second, dsecond_low)
    second_pack = jnp.concatenate(
        [
            piece
            for grad in (grad_second_up, grad_second_down)
            for piece in jnp.split(
                grad.astype(bf16).reshape(shards, -1, grad.shape[1]), grad.shape[1] // width, axis=2
            )
        ],
        axis=1,
    )
    second_shard = lax.psum_scatter(second_pack, "fsdp", scatter_dimension=0, tiled=True)
    second_sum = lax.psum(second_shard[0], "ctx")
    up_rows = second_up.shape[0]
    up_blocks = second_up.shape[1] // width
    second_up_sum = jnp.concatenate(
        [second_sum[i * up_rows : (i + 1) * up_rows] for i in range(up_blocks)], axis=1
    ).astype(jnp.float32)
    second_down_sum = second_sum[up_rows * up_blocks :].astype(jnp.float32)

    dconv_stream = dsecond_stream + dtemp
    dconv_low = dconv_stream.astype(bf16)
    dshift = product_right(dconv_low, whole_pointwise_out).reshape(depth.shape) * swish_slope(
        shifted
    )
    own_shift = jnp.sum(dshift, axis=1)
    own_cross = jnp.sum(dshift * unit_bn, axis=1)
    channel = jnp.concatenate([own_shift, own_cross], axis=0)
    channel_rows = -(-channel.shape[0] // 8) * 8
    channel = jnp.pad(channel, ((0, channel_rows - channel.shape[0]), (0, 0)))
    channel = channel_merge(channel, merge_sums, 3)
    sum_shift = channel[:micro_count][:, None, :]
    sum_cross = channel[micro_count : 2 * micro_count][:, None, :]
    ddepth = (
        inverse_bn
        * gain_rows[5]
        * (dshift - mask_micro * sum_shift / count - mask_micro * unit_bn * sum_cross / count)
    ).reshape(batch, local, width)
    dlow, dhigh = edges(ddepth.astype(bf16), HALO)
    dgated, tap_grads = depth_back(padded, dlow, dhigh, ddepth, tap_weights, taps)
    dgated = dgated.reshape(rows, width) * mask
    dexpanded = jnp.concatenate(
        [dgated * gate_sigma, dgated * linear * gate_sigma * (1.0 - gate_sigma)], axis=1
    ).astype(bf16)
    dtemp, gain_conv = norm_back(
        product_right(dexpanded, whole_pointwise_in), unit_conv, inverse_conv, gain_rows[2]
    )
    dattend_stream = dconv_stream + dtemp
    dattend_low = dattend_stream.astype(bf16)
    dcontext = product_right(dattend_low, whole_project_out).astype(bf16)
    dquery, dkeyvals, dheads = attend_back(
        start, lengths_flat, head_terms, queries, keyvals, dcontext.reshape(batch, local, width)
    )
    splits = dkeyvals.shape[0] // 2
    dkeyvals = dkeyvals.reshape(splits, 2, rows, 2 * width)
    (dkeyvals,) = scatter([dkeyvals], "ctx", None, bf16, 4)
    dtriple = jnp.concatenate([dquery.reshape(rows, width), dkeyvals], axis=1)
    dtemp, gain_attend = norm_back(
        product_right(dtriple, whole_project_in), unit_attend, inverse_attend, gain_rows[1]
    )
    dfirst_stream = dattend_stream + dtemp
    dfirst_low = (0.5 * dfirst_stream).astype(bf16)
    dup_first = (product_right(dfirst_low, whole_first_down) * swish_slope(up_first)).astype(bf16)
    dtemp, gain_first = norm_back(
        product_right(dup_first, whole_first_up), unit_first, inverse_first, gain_rows[0]
    )
    grad_tokens = (dfirst_stream + dtemp).astype(bf16).reshape(tokens.shape)

    small_grads = jnp.concatenate(
        [
            jnp.sum(tap_grads, axis=0)[:taps],
            jnp.stack([gain_first, gain_attend, gain_conv, gain_second, gain_out]),
            jnp.sum(own_cross, axis=0, keepdims=True),
            jnp.sum(own_shift, axis=0, keepdims=True),
        ],
        axis=0,
    ).T
    head_row = jnp.sum(dheads, axis=(0, 2)).reshape(1, 1, 2 * H)
    shard_rows = width // shards
    head_block = jnp.pad(
        jnp.broadcast_to(head_row, (shards, 1, 2 * H)),
        ((0, 0), (0, shard_rows - 1), (small_width // 2, small_width // 2 - 2 * H)),
    ).reshape(width, small_width)
    small_block = jnp.pad(small_grads, ((0, 0), (0, small_width - small_cols))) + head_block
    grads = [
        product_left(act_first, dfirst_low),
        product_left(normed_first, dup_first),
        product_left(normed_attend, dtriple),
        product_left(normed_conv, dexpanded),
        product_left(context, dattend_low),
        product_left(act_conv, dconv_low),
        small_block,
    ]
    blocks = [
        g.astype(bf16).reshape(shards // 2, 2, g.shape[0] // shards, g.shape[1]) for g in grads
    ]
    (
        grad_first_down,
        grad_first_up,
        grad_project_in,
        grad_pointwise_in,
        grad_project_out,
        grad_pointwise_out,
        small_sum,
    ) = scatter(blocks, "fsdp", "ctx", jnp.float32, 5)
    heads_at = small_width // 2
    return (
        output,
        grad_tokens,
        grad_first_up,
        grad_first_down,
        grad_project_in,
        grad_project_out,
        grad_pointwise_in,
        small_sum[:, :taps],
        grad_pointwise_out,
        second_up_sum,
        second_down_sum,
        small_sum[:, taps : taps + gain_count].T,
        small_sum[:, taps + gain_count],
        small_sum[0, heads_at : heads_at + 2 * H].reshape(2, H),
    )


def solution(mesh):
    in_specs = (
        P(None, "fsdp", "ctx", None),
        P(None, "fsdp"),
        P(None, "fsdp", "ctx", None),
        P("fsdp", None),
        P("fsdp", None),
        P("fsdp", None),
        P("fsdp", None),
        P("fsdp", None),
        P("fsdp", None),
        P("fsdp", None),
        P("fsdp", None),
        P("fsdp", None),
        P(None, "fsdp"),
        P("fsdp"),
        P(),
    )
    out_specs = (
        P(None, "fsdp", "ctx", None),
        P(None, "fsdp", "ctx", None),
        P("fsdp", None),
        P("fsdp", None),
        P("fsdp", None),
        P("fsdp", None),
        P("fsdp", None),
        P("fsdp", None),
        P("fsdp", None),
        P("fsdp", None),
        P("fsdp", None),
        P(None, "fsdp"),
        P("fsdp"),
        P(),
    )
    return jax.shard_map(
        per_device, mesh=mesh, in_specs=in_specs, out_specs=out_specs, check_vma=False
    )
```

```python
import functools

import jax
import jax.numpy as jnp
from jax import lax
from jax.experimental import pallas as pl
from jax.experimental.pallas import tpu as pltpu
from jax.sharding import PartitionSpec as P

H = 8
HD = 64
RFAR = 256
HALO = 16
VMEM_LIMIT = 60 * 1024 * 1024


EPS = 1e-05
NEGATIVE = -1e30
MESH = pl.DeviceIdType.MESH
ANY = pl.BlockSpec(memory_space=pl.ANY)
VMEM = pl.BlockSpec(memory_space=pltpu.VMEM)
SMEM = pl.BlockSpec(memory_space=pltpu.SMEM)


def rotated(index, step, count):
    return lax.rem(index + step + count, count)


def other_of(index):
    return index + 1 - 2 * lax.rem(index, 2)


def greet(peers):
    barrier = pltpu.get_barrier_semaphore()
    for peer in peers:
        pl.semaphore_signal(barrier, inc=1, device_id=peer, device_id_type=MESH)
    pl.semaphore_wait(barrier, len(peers))


def send(src, dst, send_sem, recv_sem, to):
    return pltpu.make_async_remote_copy(
        src_ref=src,
        dst_ref=dst,
        send_sem=send_sem,
        recv_sem=recv_sem,
        device_id=to,
        device_id_type=MESH,
    )


def steps(first, last, body):
    def step(i, carry):
        body(i)
        return carry

    lax.fori_loop(first, last, step, 0)


def dma(*shape):
    return pltpu.SemaphoreType.DMA(shape)


def staged(count, stages):
    return [
        functools.partial(stage, step - index)
        for step in range(count + len(stages) - 1)
        for index, stage in enumerate(stages)
        if 0 <= step - index < count
    ]


class Gather:
    def __init__(self, arrays, axis, pair=None, shares=None):
        self.inputs, self.axis, self.pair = arrays, axis, pair
        count, size = len(arrays), lax.axis_size(axis)
        places = 1 if pair is None else lax.axis_size(pair) // 2
        self.size, self.places = size, places
        self.used = [places if shares and shares[a] else 1 for a in range(count)]
        highs, most = size // 2, max(self.used)
        self.in_specs = [VMEM] * count
        self.out_specs = [ANY] * count
        self.outputs = [jax.ShapeDtypeStruct((size,) + a.shape, a.dtype) for a in arrays]
        self.scratch = [dma(count)] + [dma(count, highs)] * 4
        if pair is not None:
            self.scratch += [dma(count, size, most)] * 2
            self.scratch += [dma(count, size, most)] * 2

    def bind(self, ins, outs, scratch):
        axis, pair, size, places, used = self.axis, self.pair, self.size, self.places, self.used
        count = len(ins)
        keep, zs, zr, ys, yr = scratch[:5]
        me = lax.axis_index(axis)
        highs = size // 2
        low, high = lax.rem(me, 2), lax.div(me, 2)
        partner = other_of(me)
        self.peers = {(axis, d): {axis: 2 * rotated(high, d, highs) + low} for d in range(1, highs)}
        self.peers[axis, 0] = {axis: partner}
        if pair is not None:
            cs, cr, xs, xr = scratch[5:]
            spot = lax.axis_index(pair)
            side, place = lax.rem(spot, 2), lax.div(spot, 2)
            pair_to = {pair: other_of(spot)}
            self.peers[pair, 0] = pair_to
            if max(used) > 1:
                for e in range(1, places):
                    self.peers[pair, e] = {pair: 2 * rotated(place, e, places) + side}

        def part(a, ref, at=None, mine=True):
            if pair is None:
                return ref
            width = ref.shape[-1] // (2 * used[a])
            if at is None:
                at = place if used[a] > 1 else 0
            index = 2 * at + (side if mine else 1 - side)
            return ref.at[:, pl.ds(pl.multiple_of(index * width, width), width)]

        def origin(d):
            return 2 * rotated(high, -d, highs)

        def along(a, d, landed=False):
            spot_to = origin(d) + low if landed else me
            return send(
                part(a, ins[a]),
                part(a, outs[a].at[spot_to]),
                zs.at[a, d],
                zr.at[a, d],
                {axis: 2 * rotated(high, d, highs) + low},
            )

        def across_first(a, landed=False):
            return send(
                part(a, ins[a]),
                part(a, outs[a].at[partner if landed else me]),
                ys.at[a, 0],
                yr.at[a, 0],
                {axis: partner},
            )

        def across(a, d, landed=False):
            return send(
                part(a, outs[a].at[origin(d) + low]),
                part(a, outs[a].at[origin(d) + (1 - low if landed else low)]),
                ys.at[a, d],
                yr.at[a, d],
                {axis: partner},
            )

        def slot(a):
            return place if used[a] > 1 else 0

        def over(a, block, e, landed=False):
            at = rotated(place, -e, places) if landed else place
            return send(
                part(a, outs[a].at[block]),
                part(a, outs[a].at[block], at),
                xs.at[a, block, e],
                xr.at[a, block, e],
                {pair: 2 * rotated(place, e, places) + side},
            )

        def hand(a, block, at, landed=False):
            return send(
                part(a, outs[a].at[block], at),
                part(a, outs[a].at[block], at, not landed),
                cs.at[a, block, at],
                cr.at[a, block, at],
                pair_to,
            )

        def local(a):
            return pltpu.make_async_copy(ins[a], outs[a].at[me], keep.at[a])

        def spread(a, block):
            if pair is not None:
                for e in range(1, used[a]):
                    over(a, block, e).start()
                hand(a, block, slot(a)).start()

        def start():
            for a in range(count):
                steps(1, highs, lambda d: along(a, d).start())
                across_first(a).start()
            for a in range(count):
                local(a).start()

        def first(a):
            def one(d):
                along(a, d, True).wait_recv()
                across(a, d).start()
                spread(a, origin(d) + low)

            steps(1, highs, one)

        def second(a):
            across_first(a, True).wait_recv()
            spread(a, partner)

            def one(d):
                across(a, d, True).wait_recv()
                spread(a, origin(d) + 1 - low)

            steps(1, highs, one)

        def third(a):
            for e in range(1, used[a]):

                def one(i):
                    block = rotated(me, i, size)
                    over(a, block, e, True).wait_recv()
                    hand(a, block, rotated(place, -e, places)).start()

                steps(1, size, one)

        def finish():
            for a in range(count):
                if pair is not None:
                    for e in range(used[a]):
                        at = rotated(place, -e, places) if used[a] > 1 else 0
                        steps(1, size, lambda i: hand(a, rotated(me, i, size), at, True).wait_recv())
                        steps(1, size, lambda i: hand(a, rotated(me, i, size), at).wait_send())
                        if e > 0:
                            steps(1, size, lambda i: over(a, rotated(me, i, size), e).wait_send())
                steps(1, highs, lambda d: along(a, d).wait_send())
                across_first(a).wait_send()
                steps(1, highs, lambda d: across(a, d).wait_send())
                local(a).wait()

        self.start, self.finish = start, finish
        self.steps = staged(count, [first, second, third] if max(used) > 1 else [first, second])


class Scatter:
    def __init__(self, arrays, axis, pair, dtype):
        self.inputs, self.axis, self.pair = arrays, axis, pair
        count = len(arrays)
        self.size = 1 if axis is None else lax.axis_size(axis)
        self.pair_size = 1 if pair is None else lax.axis_size(pair)
        highs, places = self.size // 2, self.pair_size // 2
        split = 1 if pair is None else 2
        low_type = jnp.bfloat16
        tail = [(a.shape[-2], a.shape[-1] // split) for a in arrays]
        self.in_specs = [VMEM] * count
        self.out_specs = [VMEM] * count
        self.outputs = [jax.ShapeDtypeStruct(a.shape[-2:], dtype) for a in arrays]
        self.scratch = []
        if pair is not None:
            leads = () if axis is None else (highs, 2)
            self.scratch += [pltpu.VMEM(leads + t, low_type) for t in tail]
            self.scratch += [pltpu.VMEM((places,) + t, low_type) for t in tail]
            self.scratch += [dma(count)] * 2 + [dma(count, places)] * 2 + [dma(count)] * 2
        if axis is not None:
            self.scratch += [pltpu.VMEM((highs,) + t, low_type) for t in tail]
            self.scratch += [pltpu.VMEM((highs - 1,) + t, low_type) for t in tail]
            self.scratch += [dma(count)] * 2 + [dma(count, highs)] * 2

    def bind(self, ins, outs, scratch):
        axis, pair, size, places = self.axis, self.pair, self.size, self.pair_size // 2
        count = len(ins)
        self.peers = {}
        halves = ins
        if pair is not None:
            halves, cross = scratch[:count], scratch[count : 2 * count]
            cs, cr, xs, xr, fs, fr = scratch[2 * count : 2 * count + 6]
            scratch = scratch[2 * count + 6 :]
            spot = lax.axis_index(pair)
            side, place = lax.rem(spot, 2), lax.div(spot, 2)
            pair_to = {pair: other_of(spot)}
            self.peers[pair, 0] = pair_to
            for e in range(1, places):
                self.peers[pair, e] = {pair: 2 * rotated(place, e, places) + side}
        if axis is not None:
            lows, highs_in = scratch[:count], scratch[count : 2 * count]
            ys, yr, zs, zr = scratch[2 * count :]
            me = lax.axis_index(axis)
            highs = size // 2
            low, high = lax.rem(me, 2), lax.div(me, 2)
            partner = {axis: other_of(me)}
            for d in range(1, highs):
                self.peers[axis, d] = {axis: 2 * rotated(high, d, highs) + low}
            self.peers[axis, 0] = partner

        def columns(a, mine):
            width = halves[a].shape[-1]
            return pl.ds(pl.multiple_of((side if mine else 1 - side) * width, width), width)

        def first(a):
            theirs = columns(a, False)
            piece = ins[a].at[:, theirs] if axis is None else ins[a].at[:, :, :, theirs]
            return send(piece, halves[a], cs.at[a], cr.at[a], pair_to)

        def across(a):
            return send(halves[a].at[:, 1 - low], lows[a], ys.at[a], yr.at[a], partner)

        def along(a, d):
            to = rotated(high, d, highs)
            return send(
                lows[a].at[to],
                highs_in[a].at[d - 1],
                zs.at[a, d - 1],
                zr.at[a, d - 1],
                {axis: 2 * to + low},
            )

        def over(a, e, landed=False):
            slot = rotated(place, -e, places) if landed else place
            return send(
                cross[a].at[place],
                cross[a].at[slot],
                xs.at[a, e - 1],
                xr.at[a, e - 1],
                {pair: 2 * rotated(place, e, places) + side},
            )

        def final(a, landed=False):
            return send(
                outs[a].at[:, columns(a, True)],
                outs[a].at[:, columns(a, not landed)],
                fs.at[a],
                fr.at[a],
                pair_to,
            )

        def wide(value):
            return value.astype(jnp.float32)

        def stage_first(a):
            first(a).wait_recv()
            if axis is None:
                total = wide(ins[a][:, columns(a, True)]) + wide(halves[a][...])
                cross[a][place] = total.astype(jnp.bfloat16)
                for e in range(1, places):
                    over(a, e).start()
                return

            def one(i):
                for j in range(2):
                    own = wide(ins[a][i, j, :, columns(a, True)])
                    halves[a][i, j] = (own + wide(halves[a][i, j])).astype(jnp.bfloat16)

            steps(0, highs, one)
            across(a).start()

        def stage_across(a):
            across(a).wait_recv()

            def one(i):
                lows[a][i] = (wide(halves[a][i, low]) + wide(lows[a][i])).astype(jnp.bfloat16)

            steps(0, highs, one)
            steps(1, highs, lambda d: along(a, d).start())

        def stage_along(a):
            steps(1, highs, lambda d: along(a, d).wait_recv())

            def added(d, total):
                return total + wide(highs_in[a][d - 1])

            total = lax.fori_loop(1, highs, added, wide(lows[a][high]))
            if pair is None:
                outs[a][...] = total.astype(outs[a].dtype)
                return
            cross[a][place] = total.astype(jnp.bfloat16)
            for e in range(1, places):
                over(a, e).start()

        def stage_over(a):
            for e in range(1, places):
                over(a, e, True).wait_recv()
            total = wide(cross[a][0])
            for i in range(1, places):
                total = total + wide(cross[a][i])
            outs[a][:, columns(a, True)] = total
            final(a).start()

        def start():
            for a in range(count):
                (across(a) if pair is None else first(a)).start()

        def finish():
            for a in range(count):
                if axis is not None:
                    across(a).wait_send()
                    steps(1, highs, lambda d: along(a, d).wait_send())
                if pair is not None:
                    first(a).wait_send()
                    for e in range(1, places):
                        over(a, e).wait_send()
                    final(a, True).wait_recv()
                    final(a).wait_send()

        middle = [] if axis is None else [stage_across, stage_along]
        stages = middle if pair is None else [stage_first] + middle + [stage_over]
        self.start, self.finish, self.steps = start, finish, staged(count, stages)


def merge_sums(parts):
    total = parts[0]
    for part in parts[1:]:
        total = total + part
    return total


def merge_moments(micro, parts):
    total = merge_sums(parts)
    sums, squares, counts = (slice(i * micro, (i + 1) * micro) for i in range(3))
    mean = total[sums] / jnp.maximum(total[counts], 1.0)
    spread = total[squares]
    for part in parts:
        shift = part[sums] / jnp.maximum(part[counts], 1.0) - mean
        spread = spread + part[counts] * shift * shift
    return jnp.concatenate([total[sums], spread, total[counts], total[3 * micro :]], axis=0)


class Channels:
    def __init__(self, rows, merge):
        self.inputs, self.merge = [rows], merge
        self.axes = ("ctx", "fsdp")
        self.sizes = tuple(lax.axis_size(axis) for axis in self.axes)
        self.in_specs, self.out_specs = [VMEM], [VMEM]
        self.outputs = [jax.ShapeDtypeStruct(rows.shape, rows.dtype)]
        self.scratch = [pltpu.VMEM((size,) + rows.shape, rows.dtype) for size in self.sizes]
        self.scratch.append(pltpu.VMEM(rows.shape, rows.dtype))
        for size in self.sizes:
            self.scratch += [dma(size), dma(size)]

    def bind(self, ins, outs, scratch):
        slots, sums, sems = scratch[:2], scratch[2], scratch[3:]
        self.peers = {}
        for axis, size in zip(self.axes, self.sizes):
            me = lax.axis_index(axis)
            low, high, highs = lax.rem(me, 2), lax.div(me, 2), size // 2
            for d in range(1, highs):
                self.peers[axis, d] = {axis: 2 * rotated(high, d, highs) + low}
            self.peers[axis, 0] = {axis: other_of(me)}
            for d in range(1, highs):
                self.peers[axis, -d] = {axis: 2 * rotated(high, d, highs) + 1 - low}

        def source(stage):
            return ins[0] if stage == 0 else sums

        def copy(stage, d, landed=False):
            axis, size = self.axes[stage], self.sizes[stage]
            me = lax.axis_index(axis)
            return send(
                source(stage),
                slots[stage].at[rotated(me, -d, size) if landed else me],
                sems[2 * stage].at[d],
                sems[2 * stage + 1].at[d],
                {axis: rotated(me, d, size)},
            )

        def begin(stage):
            for d in range(1, self.sizes[stage]):
                copy(stage, d).start()
            slots[stage][lax.axis_index(self.axes[stage])] = source(stage)[...]

        def end(stage):
            for d in range(1, self.sizes[stage]):
                copy(stage, d, True).wait_recv()
            total = self.merge([slots[stage][i] for i in range(self.sizes[stage])])
            (sums if stage == 0 else outs[0])[...] = total

        def finish():
            for stage in range(2):
                for d in range(1, self.sizes[stage]):
                    copy(stage, d).wait_send()

        def middle():
            end(0)
            begin(1)

        self.start, self.finish = lambda: begin(0), finish
        self.steps = [middle, lambda: end(1)]


def exchange_kernel(jobs, *refs):
    kinds = ([len(j.inputs) for j in jobs], [len(j.outputs) for j in jobs])
    kinds += ([len(j.scratch) for j in jobs],)
    at, cuts = 0, []
    for lengths in kinds:
        row = []
        for length in lengths:
            row.append(refs[at : at + length])
            at += length
        cuts.append(row)
    peers = {}
    for job, ins, outs, scratch in zip(jobs, *cuts):
        job.bind(ins, outs, scratch)
        peers.update(job.peers)
    greet(list(peers.values()))
    for job in jobs:
        job.start()
    for turn in range(max(len(job.steps) for job in jobs)):
        for job in jobs:
            if turn < len(job.steps):
                job.steps[turn]()
    for job in jobs:
        job.finish()


def exchange(jobs, ident):
    def joined(field):
        return [entry for job in jobs for entry in getattr(job, field)]

    results = pl.pallas_call(
        functools.partial(exchange_kernel, jobs),
        out_shape=joined("outputs"),
        in_specs=joined("in_specs"),
        out_specs=joined("out_specs"),
        scratch_shapes=joined("scratch"),
        compiler_params=pltpu.CompilerParams(
            collective_id=ident, has_side_effects=True, vmem_limit_bytes=VMEM_LIMIT
        ),
        name="exchange_" + str(ident),
    )(*joined("inputs"))
    cuts, at = [], 0
    for job in jobs:
        cuts.append(results[at : at + len(job.outputs)])
        at += len(job.outputs)
    return cuts


def positions(start, rows, keys):
    query = start + lax.broadcasted_iota(jnp.int32, (rows, keys), 0)
    key = lax.broadcasted_iota(jnp.int32, (rows, keys), 1)
    offset = query - key
    distance = jnp.abs(offset).astype(jnp.float32)
    far = (offset >= RFAR).astype(jnp.float32)
    return distance, far, key


def head_probs(query, keys, terms_ref, head, distance, far, valid):
    scores = lax.dot_general(
        query, keys, (((1,), (1,)), ((), ())), preferred_element_type=jnp.float32
    )
    bias = far * terms_ref[1, head] - distance * terms_ref[0, head]
    scores = jnp.where(valid, scores * HD ** (-0.5) + bias, NEGATIVE)
    top = jnp.max(scores, axis=-1, keepdims=True)
    raised = jnp.exp(scores - top)
    return raised / jnp.sum(raised, axis=-1, keepdims=True)


def attend_kernel(start_ref, lengths_ref, terms_ref, q_ref, kv_ref, out_ref):
    rows, width = q_ref.shape[1:]
    keys = kv_ref.shape[0] * kv_ref.shape[2]
    distance, far, key = positions(start_ref[0], rows, keys)
    valid = key < lengths_ref[pl.program_id(0)]
    for head in range(H):
        cols = slice(head * HD, (head + 1) * HD)
        key_head = kv_ref[:, 0, :, cols].reshape(keys, HD)
        value_head = kv_ref[:, 0, :, width + head * HD : width + (head + 1) * HD].reshape(keys, HD)
        probs = head_probs(q_ref[0, :, cols], key_head, terms_ref, head, distance, far, valid)
        context = jnp.dot(
            probs.astype(jnp.bfloat16), value_head, preferred_element_type=jnp.float32
        )
        out_ref[0, :, cols] = context.astype(jnp.bfloat16)


def attend_back_kernel(
    start_ref, lengths_ref, terms_ref, q_ref, kv_ref, dctx_ref, dq_ref, dkv_ref, heads_ref
):
    rows, width = q_ref.shape[1:]
    shards, _, local, _ = kv_ref.shape
    keys = shards * local
    distance, far, key = positions(start_ref[0], rows, keys)
    valid = key < lengths_ref[pl.program_id(0)]
    factor = HD ** (-0.5)
    for head in range(H):
        cols = slice(head * HD, (head + 1) * HD)
        value_cols = slice(width + head * HD, width + (head + 1) * HD)
        query = q_ref[0, :, cols]
        key_head = kv_ref[:, 0, :, cols].reshape(keys, HD)
        value_head = kv_ref[:, 0, :, value_cols].reshape(keys, HD)
        dcontext = dctx_ref[0, :, cols]
        probs = head_probs(query, key_head, terms_ref, head, distance, far, valid)
        dprobs = lax.dot_general(
            dcontext, value_head, (((1,), (1,)), ((), ())), preferred_element_type=jnp.float32
        )
        dscores = probs * (dprobs - jnp.sum(probs * dprobs, axis=-1, keepdims=True))
        heads_ref[0, head : head + 1, :] = -jnp.sum(dscores * distance, axis=0, keepdims=True)
        heads_ref[0, H + head : H + head + 1, :] = jnp.sum(dscores * far, axis=0, keepdims=True)
        low = dscores.astype(jnp.bfloat16)
        dquery = jnp.dot(low, key_head, preferred_element_type=jnp.float32) * factor
        dq_ref[0, :, cols] = dquery.astype(jnp.bfloat16)
        dkey = (
            lax.dot_general(low, query, (((0,), (0,)), ((), ())), preferred_element_type=jnp.float32)
            * factor
        )
        dvalue = lax.dot_general(
            probs.astype(jnp.bfloat16),
            dcontext,
            (((0,), (0,)), ((), ())),
            preferred_element_type=jnp.float32,
        )
        dkv_ref[:, 0, :, cols] = dkey.astype(jnp.bfloat16).reshape(shards, local, HD)
        dkv_ref[:, 0, :, value_cols] = dvalue.astype(jnp.bfloat16).reshape(shards, local, HD)


def attend(start, lengths, terms, queries, keyvals):
    batch, rows, width = queries.shape
    shards, _, local, double = keyvals.shape
    block = pl.BlockSpec((1, rows, width), lambda b: (b, 0, 0))
    wide = pl.BlockSpec((shards, 1, local, double), lambda b: (0, b, 0, 0))
    return pl.pallas_call(
        attend_kernel,
        grid=(batch,),
        out_shape=jax.ShapeDtypeStruct(queries.shape, jnp.bfloat16),
        in_specs=[SMEM, SMEM, SMEM, block, wide],
        out_specs=block,
        compiler_params=pltpu.CompilerParams(vmem_limit_bytes=VMEM_LIMIT),
        name="attend",
    )(start, lengths, terms, queries, keyvals)


def attend_back(start, lengths, terms, queries, keyvals, dcontext):
    batch, rows, width = queries.shape
    shards, _, local, double = keyvals.shape
    keys = shards * local
    block = pl.BlockSpec((1, rows, width), lambda b: (b, 0, 0))
    wide = pl.BlockSpec((shards, 1, local, double), lambda b: (0, b, 0, 0))
    heads = pl.BlockSpec((1, 2 * H, keys), lambda b: (b, 0, 0))
    return pl.pallas_call(
        attend_back_kernel,
        grid=(batch,),
        out_shape=[
            jax.ShapeDtypeStruct(queries.shape, jnp.bfloat16),
            jax.ShapeDtypeStruct(keyvals.shape, jnp.bfloat16),
            jax.ShapeDtypeStruct((batch, 2 * H, keys), jnp.float32),
        ],
        in_specs=[SMEM, SMEM, SMEM, block, wide, block],
        out_specs=[block, wide, heads],
        compiler_params=pltpu.CompilerParams(vmem_limit_bytes=VMEM_LIMIT),
        name="attend_back",
    )(start, lengths, terms, queries, keyvals, dcontext)


def depth_kernel(taps, padded_ref, weight_ref, out_ref, wide):
    rows = out_ref.shape[1]
    wide[...] = padded_ref[0].astype(jnp.float32)
    shift = HALO - taps // 2
    total = wide[shift : shift + rows, :] * weight_ref[0:1, :]
    for tap in range(1, taps):
        total = total + wide[shift + tap : shift + tap + rows, :] * weight_ref[tap : tap + 1, :]
    out_ref[0] = total


def depth_back_kernel(
    taps, padded_ref, dlow_ref, dhigh_ref, ddepth_ref, weight_ref, dgated_ref, grad_ref, wide, dwide
):
    rows = ddepth_ref.shape[1]
    wide[...] = padded_ref[0].astype(jnp.float32)
    ddepth = ddepth_ref[0]
    dwide[0:HALO, :] = dlow_ref[0].astype(jnp.float32)
    dwide[HALO : HALO + rows, :] = ddepth
    dwide[HALO + rows :, :] = dhigh_ref[0].astype(jnp.float32)
    half = taps // 2
    total = jnp.zeros_like(ddepth)
    for tap in range(taps):
        at = HALO + half - tap
        total = total + dwide[at : at + rows, :] * weight_ref[tap : tap + 1, :]
        at = HALO - half + tap
        grad_ref[0, tap : tap + 1, :] = jnp.sum(
            wide[at : at + rows, :] * ddepth, axis=0, keepdims=True
        )
    grad_ref[0, taps:, :] = jnp.zeros_like(grad_ref[0, taps:, :])
    dgated_ref[0] = total


def lanes(rows, width):
    return pl.BlockSpec((1, rows, 128), lambda b, c: (b, 0, c))


def depth_apply(padded, weights, taps):
    batch, span, width = padded.shape
    rows = span - 2 * HALO
    weight = pl.BlockSpec((weights.shape[0], 128), lambda b, c: (0, c))
    return pl.pallas_call(
        functools.partial(depth_kernel, taps),
        grid=(batch, width // 128),
        out_shape=jax.ShapeDtypeStruct((batch, rows, width), jnp.float32),
        in_specs=[lanes(span, width), weight],
        out_specs=lanes(rows, width),
        scratch_shapes=[pltpu.VMEM((span, 128), jnp.float32)],
        name="depth_apply",
    )(padded, weights)


def depth_back(padded, dlow, dhigh, ddepth, weights, taps):
    batch, span, width = padded.shape
    rows = span - 2 * HALO
    padded_taps = weights.shape[0]
    weight = pl.BlockSpec((padded_taps, 128), lambda b, c: (0, c))
    return pl.pallas_call(
        functools.partial(depth_back_kernel, taps),
        grid=(batch, width // 128),
        out_shape=[
            jax.ShapeDtypeStruct((batch, rows, width), jnp.float32),
            jax.ShapeDtypeStruct((batch, padded_taps, width), jnp.float32),
        ],
        in_specs=[
            lanes(span, width),
            lanes(HALO, width),
            lanes(HALO, width),
            lanes(rows, width),
            weight,
        ],
        out_specs=[lanes(rows, width), lanes(padded_taps, width)],
        scratch_shapes=[
            pltpu.VMEM((span, 128), jnp.float32),
            pltpu.VMEM((span, 128), jnp.float32),
        ],
        name="depth_back",
    )(padded, dlow, dhigh, ddepth, weights)


def edges(block, width):
    count = lax.axis_size("ctx")
    forward = [(i, i + 1) for i in range(count - 1)]
    backward = [(target, source) for source, target in forward]
    low = lax.ppermute(block[:, block.shape[1] - width :], "ctx", forward)
    high = lax.ppermute(block[:, :width], "ctx", backward)
    return low, high


def flat_rows(gathered):
    return [a.reshape(a.shape[0] * a.shape[1], a.shape[2]) for a in gathered]


def blocked(grad, shards):
    rows, cols = grad.shape
    return grad.astype(jnp.bfloat16).reshape(shards // 2, 2, rows // shards, cols)


def product(left, right):
    return jnp.dot(left, right, preferred_element_type=jnp.float32)


def product_left(left, right):
    return jnp.dot(left.T, right, preferred_element_type=jnp.float32)


def product_right(left, right):
    return jnp.dot(left, right.T, preferred_element_type=jnp.float32)


def swish(value):
    return value * jax.nn.sigmoid(value)


def swish_slope(value):
    sigma = jax.nn.sigmoid(value)
    return sigma * (1.0 + value * (1.0 - sigma))


def layer_norm(stream, gain):
    centred = stream - jnp.mean(stream, axis=-1, keepdims=True)
    inverse = lax.rsqrt(jnp.mean(centred * centred, axis=-1, keepdims=True) + EPS)
    unit = centred * inverse
    return ((unit * gain).astype(jnp.bfloat16), unit, inverse)


def norm_back(dnormed, unit, inverse, gain):
    scaled = dnormed * gain
    dstream = inverse * (
        scaled
        - jnp.mean(scaled, axis=-1, keepdims=True)
        - unit * jnp.mean(scaled * unit, axis=-1, keepdims=True)
    )
    return (dstream, jnp.sum(dnormed * unit, axis=0))


def per_device(
    tokens,
    lengths,
    cotangent,
    first_up,
    first_down,
    project_in,
    project_out,
    pointwise_in,
    depthwise,
    pointwise_out,
    second_up,
    second_down,
    gains,
    batch_shift,
    head_terms,
):
    micro_count, seqs, local, width = tokens.shape
    batch = micro_count * seqs
    rows = batch * local
    shards = lax.axis_size("fsdp")
    taps = depthwise.shape[1]
    tap_rows = -(-taps // 8) * 8
    gain_count = gains.shape[0]
    bf16 = jnp.bfloat16
    start = (lax.axis_index("ctx") * local).astype(jnp.int32).reshape(1)
    frame_pos = start[0] + lax.iota(jnp.int32, local)
    lengths_flat = lengths.reshape(batch)
    mask = (frame_pos[None, :] < lengths_flat[:, None]).astype(jnp.float32).reshape(rows, 1)
    mask_micro = mask.reshape(micro_count, seqs * local, 1)

    small = jnp.concatenate([depthwise, gains.T, batch_shift[:, None]], axis=1)
    small_cols = small.shape[1]
    small_width = 256
    small = jnp.pad(small, ((0, 0), (0, small_width - small_cols)))
    early = Gather(
        [first_up, small, first_down, project_in], "fsdp", "ctx", (True, False, True, False)
    )
    (gathered,) = exchange([early], 0)
    whole_first_up, whole_small, whole_first_down, whole_project_in = flat_rows(gathered)
    small_rows = whole_small[:, :small_cols].astype(jnp.float32).T
    tap_weights = jnp.pad(small_rows[:taps], ((0, tap_rows - taps), (0, 0)))
    gain_rows = small_rows[taps : taps + gain_count]
    shift_row = small_rows[taps + gain_count]

    stream_in = tokens.reshape(rows, width).astype(jnp.float32)
    normed_first, unit_first, inverse_first = layer_norm(stream_in, gain_rows[0])
    up_first = product(normed_first, whole_first_up)
    act_first = swish(up_first).astype(bf16)
    stream_first = stream_in + 0.5 * product(act_first, whole_first_down)
    normed_attend, unit_attend, inverse_attend = layer_norm(stream_first, gain_rows[1])
    triple = product(normed_attend, whole_project_in).astype(bf16)
    queries = triple[:, :width].reshape(batch, local, width)
    keyvals = Gather([triple[:, width:].reshape(batch, local, 2 * width)], "ctx")
    later = Gather([project_out, pointwise_in, pointwise_out, second_up], "fsdp", "ctx")
    ((keyvals,), gathered) = exchange([keyvals, later], 1)
    whole_project_out, whole_pointwise_in, whole_pointwise_out, whole_second_up = flat_rows(gathered)
    context = attend(start, lengths_flat, head_terms, queries, keyvals).reshape(rows, width)
    stream_attend = stream_first + product(context, whole_project_out)
    normed_conv, unit_conv, inverse_conv = layer_norm(stream_attend, gain_rows[2])
    expanded = product(normed_conv, whole_pointwise_in)
    linear = expanded[:, :width]
    gate_sigma = jax.nn.sigmoid(expanded[:, width:])
    gated_low = (linear * gate_sigma * mask).astype(bf16).reshape(batch, local, width)
    low, high = edges(gated_low, HALO)
    padded = jnp.concatenate([low, gated_low, high], axis=1)
    depth = depth_apply(padded, tap_weights, taps).reshape(micro_count, seqs * local, width)

    own_count = jnp.sum(mask_micro, axis=1)
    own_sum = jnp.sum(mask_micro * depth, axis=1)
    own_mean = own_sum / jnp.maximum(own_count, 1.0)
    own_centred = depth - own_mean[:, None, :]
    own_spread = jnp.sum(mask_micro * own_centred * own_centred, axis=1)
    moments = jnp.concatenate(
        [own_sum, own_spread, jnp.broadcast_to(own_count, own_sum.shape)], axis=0
    )
    moment_rows = -(-moments.shape[0] // 8) * 8
    moments = jnp.pad(moments, ((0, moment_rows - moments.shape[0]), (0, 0)))
    merging = Channels(moments, functools.partial(merge_moments, micro_count))
    last = Gather([second_down], "fsdp", "ctx", (True,))
    ((moments,), gathered) = exchange([merging, last], 2)
    (whole_second_down,) = flat_rows(gathered)
    count = moments[2 * micro_count : 3 * micro_count][:, None, :]
    bn_mean = moments[:micro_count][:, None, :] / count
    inverse_bn = lax.rsqrt(moments[micro_count : 2 * micro_count][:, None, :] / count + EPS)
    unit_bn = (depth - bn_mean) * inverse_bn
    shifted = unit_bn * gain_rows[5] + shift_row
    act_conv = swish(shifted).astype(bf16).reshape(rows, width)
    stream_conv = stream_attend + product(act_conv, whole_pointwise_out)
    normed_second, unit_second, inverse_second = layer_norm(stream_conv, gain_rows[3])
    up_second = product(normed_second, whole_second_up)
    act_second = swish(up_second).astype(bf16)
    stream_second = stream_conv + 0.5 * product(act_second, whole_second_down)
    out_low, unit_out, inverse_out = layer_norm(stream_second, gain_rows[4])
    output = out_low.reshape(tokens.shape)

    dout = cotangent.reshape(rows, width).astype(jnp.float32)
    dsecond_stream, gain_out = norm_back(dout, unit_out, inverse_out, gain_rows[4])
    dsecond_low = (0.5 * dsecond_stream).astype(bf16)
    dup_second = (product_right(dsecond_low, whole_second_down) * swish_slope(up_second)).astype(
        bf16
    )
    dtemp, gain_second = norm_back(
        product_right(dup_second, whole_second_up), unit_second, inverse_second, gain_rows[3]
    )
    grad_second_up = product_left(normed_second, dup_second)
    grad_second_down = product_left(act_second, dsecond_low)
    second_parts = [
        lax.psum_scatter(
            grad.astype(bf16).reshape(shards, -1, grad.shape[1]),
            "fsdp",
            scatter_dimension=0,
            tiled=True,
        )[0]
        for grad in (grad_second_down, grad_second_up)
    ]

    dconv_stream = dsecond_stream + dtemp
    dconv_low = dconv_stream.astype(bf16)
    dshift = product_right(dconv_low, whole_pointwise_out).reshape(depth.shape) * swish_slope(
        shifted
    )
    own_shift = jnp.sum(dshift, axis=1)
    own_cross = jnp.sum(dshift * unit_bn, axis=1)
    channel = jnp.concatenate([own_shift, own_cross], axis=0)
    channel_rows = -(-channel.shape[0] // 8) * 8
    channel = jnp.pad(channel, ((0, channel_rows - channel.shape[0]), (0, 0)))
    ((channel,),) = exchange([Channels(channel, merge_sums)], 3)
    sum_shift = channel[:micro_count][:, None, :]
    sum_cross = channel[micro_count : 2 * micro_count][:, None, :]
    ddepth = (
        inverse_bn
        * gain_rows[5]
        * (dshift - mask_micro * sum_shift / count - mask_micro * unit_bn * sum_cross / count)
    ).reshape(batch, local, width)
    dlow, dhigh = edges(ddepth.astype(bf16), HALO)
    dgated, tap_grads = depth_back(padded, dlow, dhigh, ddepth, tap_weights, taps)
    dgated = dgated.reshape(rows, width) * mask
    dexpanded = jnp.concatenate(
        [dgated * gate_sigma, dgated * linear * gate_sigma * (1.0 - gate_sigma)], axis=1
    ).astype(bf16)
    dtemp, gain_conv = norm_back(
        product_right(dexpanded, whole_pointwise_in), unit_conv, inverse_conv, gain_rows[2]
    )
    dattend_stream = dconv_stream + dtemp
    dattend_low = dattend_stream.astype(bf16)
    dcontext = product_right(dattend_low, whole_project_out).astype(bf16)
    dquery, dkeyvals, dheads = attend_back(
        start, lengths_flat, head_terms, queries, keyvals, dcontext.reshape(batch, local, width)
    )
    splits = dkeyvals.shape[0] // 2
    dkeyvals = dkeyvals.reshape(splits, 2, rows, 2 * width)
    conv_grads = [
        product_left(normed_conv, dexpanded),
        product_left(act_conv, dconv_low),
        product_left(context, dattend_low),
    ]
    ((dkeyvals,), conv_sums) = exchange(
        [
            Scatter([dkeyvals], "ctx", None, bf16),
            Scatter([blocked(g, shards) for g in conv_grads], "fsdp", "ctx", jnp.float32),
        ],
        4,
    )
    grad_pointwise_in, grad_pointwise_out, grad_project_out = conv_sums
    dtriple = jnp.concatenate([dquery.reshape(rows, width), dkeyvals], axis=1)
    dtemp, gain_attend = norm_back(
        product_right(dtriple, whole_project_in), unit_attend, inverse_attend, gain_rows[1]
    )
    dfirst_stream = dattend_stream + dtemp
    dfirst_low = (0.5 * dfirst_stream).astype(bf16)
    dup_first = (product_right(dfirst_low, whole_first_down) * swish_slope(up_first)).astype(bf16)
    dtemp, gain_first = norm_back(
        product_right(dup_first, whole_first_up), unit_first, inverse_first, gain_rows[0]
    )
    grad_tokens = (dfirst_stream + dtemp).astype(bf16).reshape(tokens.shape)

    small_grads = jnp.concatenate(
        [
            jnp.sum(tap_grads, axis=0)[:taps],
            jnp.stack([gain_first, gain_attend, gain_conv, gain_second, gain_out]),
            jnp.sum(own_cross, axis=0, keepdims=True),
            jnp.sum(own_shift, axis=0, keepdims=True),
        ],
        axis=0,
    ).T
    head_row = jnp.sum(dheads, axis=(0, 2)).reshape(1, 1, 2 * H)
    shard_rows = width // shards
    head_block = jnp.pad(
        jnp.broadcast_to(head_row, (shards, 1, 2 * H)),
        ((0, 0), (0, shard_rows - 1), (small_width // 2, small_width // 2 - 2 * H)),
    ).reshape(width, small_width)
    small_block = jnp.pad(small_grads, ((0, 0), (0, small_width - small_cols))) + head_block
    grads = [
        product_left(act_first, dfirst_low),
        product_left(normed_first, dup_first),
        product_left(normed_attend, dtriple),
        small_block,
    ]
    (second_sums, sums) = exchange(
        [
            Scatter(second_parts, None, "ctx", jnp.float32),
            Scatter([blocked(g, shards) for g in grads], "fsdp", "ctx", jnp.float32),
        ],
        5,
    )
    second_down_sum, second_up_sum = second_sums
    grad_first_down, grad_first_up, grad_project_in, small_sum = sums
    heads_at = small_width // 2
    return (
        output,
        grad_tokens,
        grad_first_up,
        grad_first_down,
        grad_project_in,
        grad_project_out,
        grad_pointwise_in,
        small_sum[:, :taps],
        grad_pointwise_out,
        second_up_sum,
        second_down_sum,
        small_sum[:, taps : taps + gain_count].T,
        small_sum[:, taps + gain_count],
        small_sum[0, heads_at : heads_at + 2 * H].reshape(2, H),
    )


def solution(mesh):
    in_specs = (
        P(None, "fsdp", "ctx", None),
        P(None, "fsdp"),
        P(None, "fsdp", "ctx", None),
        P("fsdp", None),
        P("fsdp", None),
        P("fsdp", None),
        P("fsdp", None),
        P("fsdp", None),
        P("fsdp", None),
        P("fsdp", None),
        P("fsdp", None),
        P("fsdp", None),
        P(None, "fsdp"),
        P("fsdp"),
        P(),
    )
    out_specs = (
        P(None, "fsdp", "ctx", None),
        P(None, "fsdp", "ctx", None),
        P("fsdp", None),
        P("fsdp", None),
        P("fsdp", None),
        P("fsdp", None),
        P("fsdp", None),
        P("fsdp", None),
        P("fsdp", None),
        P("fsdp", None),
        P("fsdp", None),
        P(None, "fsdp"),
        P("fsdp"),
        P(),
    )
    return jax.shard_map(
        per_device, mesh=mesh, in_specs=in_specs, out_specs=out_specs, check_vma=False
    )
```

```python
import functools

import jax
import jax.numpy as jnp
from jax import lax
from jax.experimental import pallas as pl
from jax.experimental.pallas import tpu as pltpu
from jax.sharding import PartitionSpec as P

H = 8
HD = 64
RFAR = 256
HALO = 16
VMEM_LIMIT = 60 * 1024 * 1024


EPS = 1e-05
NEGATIVE = -1e30
MESH = pl.DeviceIdType.MESH
ANY = pl.BlockSpec(memory_space=pl.ANY)
VMEM = pl.BlockSpec(memory_space=pltpu.VMEM)
SMEM = pl.BlockSpec(memory_space=pltpu.SMEM)


def rotated(index, step, count):
    return lax.rem(index + step + count, count)


def other_of(index):
    return index + 1 - 2 * lax.rem(index, 2)


def greet(peers):
    barrier = pltpu.get_barrier_semaphore()
    for peer in peers:
        pl.semaphore_signal(barrier, inc=1, device_id=peer, device_id_type=MESH)
    pl.semaphore_wait(barrier, len(peers))


def send(src, dst, send_sem, recv_sem, to):
    return pltpu.make_async_remote_copy(
        src_ref=src,
        dst_ref=dst,
        send_sem=send_sem,
        recv_sem=recv_sem,
        device_id=to,
        device_id_type=MESH,
    )


UNROLL = 8
PIECE, SUM_PIECE = 64 * 1024, 64 * 512


def steps(first, last, body):
    if last - first <= UNROLL:
        for i in range(first, last):
            body(i)
        return

    def step(i, carry):
        body(i)
        return carry

    lax.fori_loop(first, last, step, 0)


def dma(*shape):
    return pltpu.SemaphoreType.DMA(shape)


def pieces_of(array, shape, least, size):
    rows, cols = shape
    want = max(1, rows * cols // size)
    across = max(k for k in range(1, want + 1) if cols % (least * k) == 0 or k == 1)
    down = max(k for k in range(1, want // across + 1) if rows % (16 * k) == 0 or k == 1)
    height, width = rows // down, cols // across
    return [
        (array, i * height, height, j * width, width) for i in range(down) for j in range(across)
    ]


def turns(index, count):
    if count > UNROLL:
        return lambda step: rotated(index, step, count)
    known = {0: index}
    for step in range(1, count):
        known[step] = rotated(index, step, count)
    return lambda step: known[step % count] if isinstance(step, int) else rotated(index, step, count)


LAG, SUM_LAG = 2, 3
AHEAD = 2


def staged(count, stages, lag):
    return [
        functools.partial(stage, step - lag * index)
        for step in range(count + lag * (len(stages) - 1))
        for index, stage in enumerate(stages)
        if 0 <= step - lag * index < count
    ]


class Gather:
    def __init__(self, arrays, axis, pair=None, shares=None):
        self.inputs, self.axis, self.pair = arrays, axis, pair
        size = lax.axis_size(axis)
        places = 1 if pair is None else lax.axis_size(pair) // 2
        self.size, self.places = size, places
        used = [places if shares and shares[a] else 1 for a in range(len(arrays))]
        sides = 1 if pair is None else 2
        self.pieces = [
            piece
            for a, array in enumerate(arrays)
            for piece in pieces_of(a, array.shape, 128 * sides * used[a], PIECE)
        ]
        self.used = [used[piece[0]] for piece in self.pieces]
        count, highs, most = len(self.pieces), size // 2, max(used)
        self.in_specs = [VMEM] * len(arrays)
        self.out_specs = [ANY] * len(arrays)
        self.outputs = [jax.ShapeDtypeStruct((size,) + a.shape, a.dtype) for a in arrays]
        self.scratch = [dma(len(arrays))] + [dma(count, highs)] * 4
        if pair is not None:
            self.scratch += [dma(count, size, most)] * 4

    def bind(self, ins, outs, scratch):
        axis, pair, size, places, used = self.axis, self.pair, self.size, self.places, self.used
        pieces = self.pieces
        count = len(pieces)
        keep, zs, zr, ys, yr = scratch[:5]
        me = lax.axis_index(axis)
        highs = size // 2
        low, high = lax.rem(me, 2), lax.div(me, 2)
        partner, other = other_of(me), 1 - low
        around, up = turns(me, size), turns(high, highs)
        self.peers = {(axis, d): {axis: 2 * up(d) + low} for d in range(1, highs)}
        self.peers[axis, 0] = {axis: partner}
        if pair is not None:
            cs, cr, xs, xr = scratch[5:]
            spot = lax.axis_index(pair)
            side, place = lax.rem(spot, 2), lax.div(spot, 2)
            beside = turns(place, places)
            pair_to = {pair: other_of(spot)}
            self.peers[pair, 0] = pair_to
            if max(used) > 1:
                for e in range(1, places):
                    self.peers[pair, e] = {pair: 2 * beside(e) + side}

        def window(p, ref, at=None, mine=True):
            _, row, rows, col, cols = pieces[p]
            if pair is None:
                return ref.at[pl.ds(row, rows), pl.ds(col, cols)]
            width = cols // (2 * used[p])
            if at is None:
                at = place if used[p] > 1 else 0
            index = 2 * at + (side if mine else 1 - side)
            start = pl.multiple_of(col + index * width, 128)
            return ref.at[pl.ds(row, rows), pl.ds(start, width)]

        def source(p):
            return window(p, ins[pieces[p][0]])

        def block(p, place, at=None, mine=True):
            return window(p, outs[pieces[p][0]].at[place], at, mine)

        def along(p, d, landed=False):
            to = 2 * up(-d) + low if landed else me
            return send(
                source(p), block(p, to), zs.at[p, d], zr.at[p, d], {axis: 2 * up(d) + low}
            )

        def across(p, d, landed=False):
            from_ref = source(p) if isinstance(d, int) and d == 0 else block(p, 2 * up(-d) + low)
            to = 2 * up(-d) + (other if landed else low)
            return send(from_ref, block(p, to), ys.at[p, d], yr.at[p, d], {axis: partner})

        def over(p, b, e, landed=False):
            at = beside(-e) if landed else place
            return send(
                block(p, b),
                block(p, b, at),
                xs.at[p, b, e],
                xr.at[p, b, e],
                {pair: 2 * beside(e) + side},
            )

        def hand(p, b, at, landed=False):
            return send(
                block(p, b, at), block(p, b, at, not landed), cs.at[p, b, at], cr.at[p, b, at], pair_to
            )

        def local(a):
            return pltpu.make_async_copy(ins[a], outs[a].at[me], keep.at[a])

        def spread(p, b):
            if pair is not None:
                for e in range(1, used[p]):
                    over(p, b, e).start()
                hand(p, b, place if used[p] > 1 else 0).start()

        def begin(p):
            if p < count:
                steps(1, highs, lambda d: along(p, d).start())
                across(p, 0).start()

        def start():
            for p in range(AHEAD):
                begin(p)
            for a in range(len(ins)):
                local(a).start()

        def first(p):
            begin(p + AHEAD)

            def one(d):
                along(p, d, True).wait_recv()
                across(p, d).start()
                spread(p, 2 * up(-d) + low)

            steps(1, highs, one)

        def second(p):
            def one(d):
                across(p, d, True).wait_recv()
                spread(p, 2 * up(-d) + other)

            one(0)
            steps(1, highs, one)

        def third(p):
            for e in range(1, used[p]):

                def one(i):
                    over(p, around(i), e, True).wait_recv()
                    hand(p, around(i), beside(-e)).start()

                steps(1, size, one)

        def finish():
            for p in range(count):
                if pair is not None:
                    for e in range(used[p]):
                        at = beside(-e) if used[p] > 1 else 0
                        steps(1, size, lambda i: hand(p, around(i), at, True).wait_recv())
                        steps(1, size, lambda i: hand(p, around(i), at).wait_send())
                        if e > 0:
                            steps(1, size, lambda i: over(p, around(i), e).wait_send())
                steps(1, highs, lambda d: along(p, d).wait_send())
                across(p, 0).wait_send()
                steps(1, highs, lambda d: across(p, d).wait_send())
            for a in range(len(ins)):
                local(a).wait()

        self.start, self.finish = start, finish
        self.steps = staged(
            count, [first, second, third] if max(used) > 1 else [first, second], LAG
        )


class Scatter:
    def __init__(self, arrays, axis, pair, dtype, shares=None):
        self.inputs, self.axis, self.pair = arrays, axis, pair
        self.size = lax.axis_size(axis)
        self.pair_size = 1 if pair is None else lax.axis_size(pair)
        highs, places = self.size // 2, self.pair_size // 2
        sides = 1 if pair is None else 2
        used = [places if shares and shares[a] else 1 for a in range(len(arrays))]
        low_type = jnp.bfloat16
        self.pieces = [
            piece
            for a, array in enumerate(arrays)
            for piece in pieces_of(a, array.shape[2:], 128 * sides * used[a], SUM_PIECE)
        ]
        self.used = [used[piece[0]] for piece in self.pieces]
        count = len(self.pieces)
        tail = [
            (rows, cols // (sides * u)) for (_, _, rows, _, cols), u in zip(self.pieces, self.used)
        ]
        self.in_specs = [VMEM] * len(arrays)
        self.out_specs = [VMEM] * len(arrays)
        self.outputs = [jax.ShapeDtypeStruct(a.shape[2:], dtype) for a in arrays]
        self.scratch = [pltpu.VMEM((highs,) + t, low_type) for t in tail]
        self.scratch += [pltpu.VMEM((highs - 1,) + t, low_type) for t in tail]
        self.scratch += [dma(count)] * 2 + [dma(count, highs)] * 2
        if pair is not None:
            wide = [(highs, 2, rows, cols * u) for (rows, cols), u in zip(tail, self.used)]
            cut = [
                (places - 1, highs, 2) + t if u > 1 else (1, 1, 1, 8, 128)
                for t, u in zip(tail, self.used)
            ]
            cross = [(1, 8, 128) if u > 1 else (places,) + t for t, u in zip(tail, self.used)]
            self.scratch += [pltpu.VMEM(t, low_type) for t in wide]
            self.scratch += [pltpu.VMEM(t, low_type) for t in cut]
            self.scratch += [pltpu.VMEM(t, low_type) for t in cross]
            self.scratch += [dma(count)] * 2 + [dma(count, places)] * 6

    def bind(self, ins, outs, scratch):
        axis, pair, size, places = self.axis, self.pair, self.size, self.pair_size // 2
        pieces, used = self.pieces, self.used
        count = len(pieces)
        lows, highs_in = scratch[:count], scratch[count : 2 * count]
        ys, yr, zs, zr = scratch[2 * count : 2 * count + 4]
        scratch = scratch[2 * count + 4 :]
        me = lax.axis_index(axis)
        highs = size // 2
        low, high = lax.rem(me, 2), lax.div(me, 2)
        up = turns(high, highs)
        partner = {axis: other_of(me)}
        self.peers = {(axis, d): {axis: 2 * up(d) + low} for d in range(1, highs)}
        self.peers[axis, 0] = partner
        if pair is not None:
            halves, cuts, cross = (scratch[i * count : (i + 1) * count] for i in range(3))
            cs, cr, xs, xr, qs, qr, fs, fr = scratch[3 * count :]
            spot = lax.axis_index(pair)
            side, place = lax.rem(spot, 2), lax.div(spot, 2)
            beside = turns(place, places)
            pair_to = {pair: other_of(spot)}
            self.peers[pair, 0] = pair_to
            for e in range(1, places):
                self.peers[pair, e] = {pair: 2 * beside(e) + side}

        def wide(value):
            return value.astype(jnp.float32)

        def each(last, body):
            def step(i, carry):
                body(i)
                return carry

            lax.fori_loop(0, last, step, 0)

        def window(p, mine=True, at=None):
            _, row, rows, col, cols = pieces[p]
            if pair is None:
                return pl.ds(row, rows), pl.ds(col, cols)
            width = cols // (2 * used[p])
            index = (side if mine else 1 - side) * used[p]
            if used[p] > 1:
                index = index + (place if at is None else at)
            return pl.ds(row, rows), pl.ds(pl.multiple_of(col + index * width, 128), width)

        def half(p, mine=True):
            _, row, rows, col, cols = pieces[p]
            start = pl.multiple_of(col + (side if mine else 1 - side) * (cols // 2), 128)
            return pl.ds(row, rows), pl.ds(start, cols // 2)

        def share(p, at):
            width = pieces[p][4] // (2 * used[p])
            return pl.ds(pl.multiple_of(at * width, 128), width)

        def first(p):
            rows, cols = half(p, False)
            piece = ins[pieces[p][0]].at[:, :, rows, cols]
            return send(piece, halves[p], cs.at[p], cr.at[p], pair_to)

        def apart(p, e):
            return send(
                halves[p].at[:, :, :, share(p, beside(e))],
                cuts[p].at[e - 1],
                qs.at[p, e],
                qr.at[p, e],
                {pair: 2 * beside(e) + side},
            )

        def across(p):
            if pair is None:
                rows, cols = window(p)
                piece = ins[pieces[p][0]].at[:, 1 - low, rows, cols]
            elif used[p] > 1:
                piece = cuts[p].at[0, :, 1 - low]
            else:
                piece = halves[p].at[:, 1 - low]
            return send(piece, lows[p], ys.at[p], yr.at[p], partner)

        def along(p, d):
            return send(
                lows[p].at[up(d)],
                highs_in[p].at[d - 1],
                zs.at[p, d - 1],
                zr.at[p, d - 1],
                {axis: 2 * up(d) + low},
            )

        def over(p, e, landed=False):
            slot = beside(-e) if landed else place
            if used[p] > 1:
                out = outs[pieces[p][0]]
                source, target = out.at[window(p)], out.at[window(p, at=slot)]
            else:
                source, target = cross[p].at[place], cross[p].at[slot]
            return send(source, target, xs.at[p, e], xr.at[p, e], {pair: 2 * beside(e) + side})

        def final(p, e=0, landed=False):
            out, at = outs[pieces[p][0]], beside(-e)
            return send(
                out.at[window(p, at=at)],
                out.at[window(p, not landed, at)],
                fs.at[p, e],
                fr.at[p, e],
                pair_to,
            )

        def stage_first(p):
            first(p).wait_recv()
            rows, cols = half(p)

            def one(i):
                for j in range(2):
                    own = wide(ins[pieces[p][0]][i, j, rows, cols])
                    halves[p][i, j] = (own + wide(halves[p][i, j])).astype(jnp.bfloat16)

            each(highs, one)
            if used[p] > 1:
                for e in range(1, places):
                    apart(p, e).start()
            else:
                across(p).start()

        def stage_apart(p):
            if used[p] == 1:
                return
            for e in range(1, places):
                apart(p, e).wait_recv()

            def one(i):
                for j in range(2):
                    total = wide(halves[p][i, j, :, share(p, place)])
                    for e in range(1, places):
                        total = total + wide(cuts[p][e - 1, i, j])
                    cuts[p][0, i, j] = total.astype(jnp.bfloat16)

            each(highs, one)
            across(p).start()

        def stage_across(p):
            across(p).wait_recv()
            rows, cols = window(p)

            def one(i):
                if pair is None:
                    own = ins[pieces[p][0]][i, low, rows, cols]
                else:
                    own = cuts[p][0, i, low] if used[p] > 1 else halves[p][i, low]
                lows[p][i] = (wide(own) + wide(lows[p][i])).astype(jnp.bfloat16)

            each(highs, one)
            steps(1, highs, lambda d: along(p, d).start())

        def stage_along(p):
            steps(1, highs, lambda d: along(p, d).wait_recv())

            def added(d, total):
                return total + wide(highs_in[p][d - 1])

            total = lax.fori_loop(1, highs, added, wide(lows[p][high]))
            out = outs[pieces[p][0]]
            if pair is None:
                out[window(p)] = total.astype(out.dtype)
                return
            if used[p] > 1:
                out[window(p)] = total
                final(p).start()
            else:
                cross[p][place] = total.astype(jnp.bfloat16)
            for e in range(1, places):
                over(p, e).start()

        def stage_over(p):
            for e in range(1, places):
                over(p, e, True).wait_recv()
                if used[p] > 1:
                    final(p, e).start()
            if used[p] == 1:
                total = wide(cross[p][0])
                for i in range(1, places):
                    total = total + wide(cross[p][i])
                outs[pieces[p][0]][window(p)] = total
                final(p).start()

        def start():
            for p in range(count):
                (across(p) if pair is None else first(p)).start()

        def finish():
            for p in range(count):
                across(p).wait_send()
                steps(1, highs, lambda d: along(p, d).wait_send())
                if pair is not None:
                    first(p).wait_send()
                    for e in range(1, places):
                        over(p, e).wait_send()
                        if used[p] > 1:
                            apart(p, e).wait_send()
                    for e in range(used[p]):
                        final(p, e, True).wait_recv()
                        final(p, e).wait_send()

        middle = [stage_across, stage_along]
        if max(used) > 1:
            middle = [stage_apart] + middle
        stages = middle if pair is None else [stage_first] + middle + [stage_over]
        self.start, self.finish, self.steps = start, finish, staged(count, stages, SUM_LAG)


def merge_sums(parts):
    total = parts[0]
    for part in parts[1:]:
        total = total + part
    return total


def merge_moments(micro, parts):
    total = merge_sums(parts)
    sums, squares, counts = (slice(i * micro, (i + 1) * micro) for i in range(3))
    mean = total[sums] / jnp.maximum(total[counts], 1.0)
    spread = total[squares]
    for part in parts:
        shift = part[sums] / jnp.maximum(part[counts], 1.0) - mean
        spread = spread + part[counts] * shift * shift
    return jnp.concatenate([total[sums], spread, total[counts], total[3 * micro :]], axis=0)


class Channels:
    def __init__(self, rows, merge):
        self.inputs, self.merge = [rows], merge
        self.axes = ("ctx", "fsdp")
        self.sizes = tuple(lax.axis_size(axis) for axis in self.axes)
        self.in_specs, self.out_specs = [VMEM], [VMEM]
        self.outputs = [jax.ShapeDtypeStruct(rows.shape, rows.dtype)]
        self.scratch = [pltpu.VMEM((size,) + rows.shape, rows.dtype) for size in self.sizes]
        self.scratch.append(pltpu.VMEM(rows.shape, rows.dtype))
        for size in self.sizes:
            self.scratch += [dma(size), dma(size)]

    def bind(self, ins, outs, scratch):
        slots, sums, sems = scratch[:2], scratch[2], scratch[3:]
        self.peers = {}
        for axis, size in zip(self.axes, self.sizes):
            me = lax.axis_index(axis)
            low, high, highs = lax.rem(me, 2), lax.div(me, 2), size // 2
            for d in range(1, highs):
                self.peers[axis, d] = {axis: 2 * rotated(high, d, highs) + low}
            self.peers[axis, 0] = {axis: other_of(me)}
            for d in range(1, highs):
                self.peers[axis, -d] = {axis: 2 * rotated(high, d, highs) + 1 - low}

        def source(stage):
            return ins[0] if stage == 0 else sums

        def copy(stage, d, landed=False):
            axis, size = self.axes[stage], self.sizes[stage]
            me = lax.axis_index(axis)
            return send(
                source(stage),
                slots[stage].at[rotated(me, -d, size) if landed else me],
                sems[2 * stage].at[d],
                sems[2 * stage + 1].at[d],
                {axis: rotated(me, d, size)},
            )

        def begin(stage):
            for d in range(1, self.sizes[stage]):
                copy(stage, d).start()
            slots[stage][lax.axis_index(self.axes[stage])] = source(stage)[...]

        def end(stage):
            for d in range(1, self.sizes[stage]):
                copy(stage, d, True).wait_recv()
            total = self.merge([slots[stage][i] for i in range(self.sizes[stage])])
            (sums if stage == 0 else outs[0])[...] = total

        def finish():
            for stage in range(2):
                for d in range(1, self.sizes[stage]):
                    copy(stage, d).wait_send()

        def middle():
            end(0)
            begin(1)

        self.start, self.finish = lambda: begin(0), finish
        self.steps = [middle, lambda: end(1)]


def exchange_kernel(jobs, *refs):
    kinds = ([len(j.inputs) for j in jobs], [len(j.outputs) for j in jobs])
    kinds += ([len(j.scratch) for j in jobs],)
    at, cuts = 0, []
    for lengths in kinds:
        row = []
        for length in lengths:
            row.append(refs[at : at + length])
            at += length
        cuts.append(row)
    peers = {}
    for job, ins, outs, scratch in zip(jobs, *cuts):
        job.bind(ins, outs, scratch)
        peers.update(job.peers)
    greet(list(peers.values()))
    for job in jobs:
        job.start()
    for turn in range(max(len(job.steps) for job in jobs)):
        for job in jobs:
            if turn < len(job.steps):
                job.steps[turn]()
    for job in jobs:
        job.finish()


def exchange(jobs, ident):
    def joined(field):
        return [entry for job in jobs for entry in getattr(job, field)]

    results = pl.pallas_call(
        functools.partial(exchange_kernel, jobs),
        out_shape=joined("outputs"),
        in_specs=joined("in_specs"),
        out_specs=joined("out_specs"),
        scratch_shapes=joined("scratch"),
        compiler_params=pltpu.CompilerParams(
            collective_id=ident, has_side_effects=True, vmem_limit_bytes=VMEM_LIMIT
        ),
        name="exchange_" + str(ident),
    )(*joined("inputs"))
    cuts, at = [], 0
    for job in jobs:
        cuts.append(results[at : at + len(job.outputs)])
        at += len(job.outputs)
    return cuts


def positions(start, rows, keys):
    query = start + lax.broadcasted_iota(jnp.int32, (rows, keys), 0)
    key = lax.broadcasted_iota(jnp.int32, (rows, keys), 1)
    offset = query - key
    distance = jnp.abs(offset).astype(jnp.float32)
    far = (offset >= RFAR).astype(jnp.float32)
    return distance, far, key


def head_probs(query, keys, terms_ref, head, distance, far, valid):
    scores = lax.dot_general(
        query, keys, (((1,), (1,)), ((), ())), preferred_element_type=jnp.float32
    )
    bias = far * terms_ref[1, head] - distance * terms_ref[0, head]
    scores = jnp.where(valid, scores * HD ** (-0.5) + bias, NEGATIVE)
    top = jnp.max(scores, axis=-1, keepdims=True)
    raised = jnp.exp(scores - top)
    return raised / jnp.sum(raised, axis=-1, keepdims=True)


def attend_kernel(start_ref, lengths_ref, terms_ref, q_ref, kv_ref, out_ref):
    rows, width = q_ref.shape[1:]
    keys = kv_ref.shape[0] * kv_ref.shape[2]
    distance, far, key = positions(start_ref[0], rows, keys)
    valid = key < lengths_ref[pl.program_id(0)]
    for head in range(H):
        cols = slice(head * HD, (head + 1) * HD)
        key_head = kv_ref[:, 0, :, cols].reshape(keys, HD)
        value_head = kv_ref[:, 0, :, width + head * HD : width + (head + 1) * HD].reshape(keys, HD)
        probs = head_probs(q_ref[0, :, cols], key_head, terms_ref, head, distance, far, valid)
        context = jnp.dot(
            probs.astype(jnp.bfloat16), value_head, preferred_element_type=jnp.float32
        )
        out_ref[0, :, cols] = context.astype(jnp.bfloat16)


def attend_back_kernel(
    start_ref, lengths_ref, terms_ref, q_ref, kv_ref, dctx_ref, dq_ref, dkv_ref, heads_ref
):
    rows, width = q_ref.shape[1:]
    shards, _, local, _ = kv_ref.shape
    keys = shards * local
    distance, far, key = positions(start_ref[0], rows, keys)
    valid = key < lengths_ref[pl.program_id(0)]
    factor = HD ** (-0.5)
    for head in range(H):
        cols = slice(head * HD, (head + 1) * HD)
        value_cols = slice(width + head * HD, width + (head + 1) * HD)
        query = q_ref[0, :, cols]
        key_head = kv_ref[:, 0, :, cols].reshape(keys, HD)
        value_head = kv_ref[:, 0, :, value_cols].reshape(keys, HD)
        dcontext = dctx_ref[0, :, cols]
        probs = head_probs(query, key_head, terms_ref, head, distance, far, valid)
        dprobs = lax.dot_general(
            dcontext, value_head, (((1,), (1,)), ((), ())), preferred_element_type=jnp.float32
        )
        dscores = probs * (dprobs - jnp.sum(probs * dprobs, axis=-1, keepdims=True))
        heads_ref[0, head : head + 1, :] = -jnp.sum(dscores * distance, axis=0, keepdims=True)
        heads_ref[0, H + head : H + head + 1, :] = jnp.sum(dscores * far, axis=0, keepdims=True)
        low = dscores.astype(jnp.bfloat16)
        dquery = jnp.dot(low, key_head, preferred_element_type=jnp.float32) * factor
        dq_ref[0, :, cols] = dquery.astype(jnp.bfloat16)
        dkey = (
            lax.dot_general(low, query, (((0,), (0,)), ((), ())), preferred_element_type=jnp.float32)
            * factor
        )
        dvalue = lax.dot_general(
            probs.astype(jnp.bfloat16),
            dcontext,
            (((0,), (0,)), ((), ())),
            preferred_element_type=jnp.float32,
        )
        dkv_ref[:, 0, :, cols] = dkey.astype(jnp.bfloat16).reshape(shards, local, HD)
        dkv_ref[:, 0, :, value_cols] = dvalue.astype(jnp.bfloat16).reshape(shards, local, HD)


def attend(start, lengths, terms, queries, keyvals):
    batch, rows, width = queries.shape
    shards, _, local, double = keyvals.shape
    block = pl.BlockSpec((1, rows, width), lambda b: (b, 0, 0))
    wide = pl.BlockSpec((shards, 1, local, double), lambda b: (0, b, 0, 0))
    return pl.pallas_call(
        attend_kernel,
        grid=(batch,),
        out_shape=jax.ShapeDtypeStruct(queries.shape, jnp.bfloat16),
        in_specs=[SMEM, SMEM, SMEM, block, wide],
        out_specs=block,
        compiler_params=pltpu.CompilerParams(vmem_limit_bytes=VMEM_LIMIT),
        name="attend",
    )(start, lengths, terms, queries, keyvals)


def attend_back(start, lengths, terms, queries, keyvals, dcontext):
    batch, rows, width = queries.shape
    shards, _, local, double = keyvals.shape
    keys = shards * local
    block = pl.BlockSpec((1, rows, width), lambda b: (b, 0, 0))
    wide = pl.BlockSpec((shards, 1, local, double), lambda b: (0, b, 0, 0))
    heads = pl.BlockSpec((1, 2 * H, keys), lambda b: (b, 0, 0))
    return pl.pallas_call(
        attend_back_kernel,
        grid=(batch,),
        out_shape=[
            jax.ShapeDtypeStruct(queries.shape, jnp.bfloat16),
            jax.ShapeDtypeStruct(keyvals.shape, jnp.bfloat16),
            jax.ShapeDtypeStruct((batch, 2 * H, keys), jnp.float32),
        ],
        in_specs=[SMEM, SMEM, SMEM, block, wide, block],
        out_specs=[block, wide, heads],
        compiler_params=pltpu.CompilerParams(vmem_limit_bytes=VMEM_LIMIT),
        name="attend_back",
    )(start, lengths, terms, queries, keyvals, dcontext)


def depth_kernel(taps, padded_ref, weight_ref, out_ref, wide):
    rows = out_ref.shape[1]
    wide[...] = padded_ref[0].astype(jnp.float32)
    shift = HALO - taps // 2
    total = wide[shift : shift + rows, :] * weight_ref[0:1, :]
    for tap in range(1, taps):
        total = total + wide[shift + tap : shift + tap + rows, :] * weight_ref[tap : tap + 1, :]
    out_ref[0] = total


def depth_back_kernel(
    taps, padded_ref, dlow_ref, dhigh_ref, ddepth_ref, weight_ref, dgated_ref, grad_ref, wide, dwide
):
    rows = ddepth_ref.shape[1]
    wide[...] = padded_ref[0].astype(jnp.float32)
    ddepth = ddepth_ref[0]
    dwide[0:HALO, :] = dlow_ref[0].astype(jnp.float32)
    dwide[HALO : HALO + rows, :] = ddepth
    dwide[HALO + rows :, :] = dhigh_ref[0].astype(jnp.float32)
    half = taps // 2
    total = jnp.zeros_like(ddepth)
    for tap in range(taps):
        at = HALO + half - tap
        total = total + dwide[at : at + rows, :] * weight_ref[tap : tap + 1, :]
        at = HALO - half + tap
        grad_ref[0, tap : tap + 1, :] = jnp.sum(
            wide[at : at + rows, :] * ddepth, axis=0, keepdims=True
        )
    grad_ref[0, taps:, :] = jnp.zeros_like(grad_ref[0, taps:, :])
    dgated_ref[0] = total


def lanes(rows, width):
    return pl.BlockSpec((1, rows, 128), lambda b, c: (b, 0, c))


def depth_apply(padded, weights, taps):
    batch, span, width = padded.shape
    rows = span - 2 * HALO
    weight = pl.BlockSpec((weights.shape[0], 128), lambda b, c: (0, c))
    return pl.pallas_call(
        functools.partial(depth_kernel, taps),
        grid=(batch, width // 128),
        out_shape=jax.ShapeDtypeStruct((batch, rows, width), jnp.float32),
        in_specs=[lanes(span, width), weight],
        out_specs=lanes(rows, width),
        scratch_shapes=[pltpu.VMEM((span, 128), jnp.float32)],
        name="depth_apply",
    )(padded, weights)


def depth_back(padded, dlow, dhigh, ddepth, weights, taps):
    batch, span, width = padded.shape
    rows = span - 2 * HALO
    padded_taps = weights.shape[0]
    weight = pl.BlockSpec((padded_taps, 128), lambda b, c: (0, c))
    return pl.pallas_call(
        functools.partial(depth_back_kernel, taps),
        grid=(batch, width // 128),
        out_shape=[
            jax.ShapeDtypeStruct((batch, rows, width), jnp.float32),
            jax.ShapeDtypeStruct((batch, padded_taps, width), jnp.float32),
        ],
        in_specs=[
            lanes(span, width),
            lanes(HALO, width),
            lanes(HALO, width),
            lanes(rows, width),
            weight,
        ],
        out_specs=[lanes(rows, width), lanes(padded_taps, width)],
        scratch_shapes=[
            pltpu.VMEM((span, 128), jnp.float32),
            pltpu.VMEM((span, 128), jnp.float32),
        ],
        name="depth_back",
    )(padded, dlow, dhigh, ddepth, weights)


def results_kernel(count, taps, gains, heads_at, *refs):
    ins, small, outs = refs[:count], refs[count], refs[count + 1 : 2 * count + 1]
    depthwise, gain_rows, shift, heads, sems = refs[2 * count + 1 :]
    copies = [pltpu.make_async_copy(ins[i], outs[i], sems.at[i]) for i in range(count)]
    for copy in copies:
        copy.start()
    turned = small[:, :128].T
    depthwise[...] = small[:, :taps]
    gain_rows[...] = turned[taps : taps + gains]
    shift[...] = turned[taps + gains : taps + gains + 1]
    heads[...] = small[0:1, heads_at : heads_at + 2 * H]
    for copy in copies:
        copy.wait()


def results(sums, small, taps, gains, heads_at):
    rows, count = small.shape[0], len(sums)
    shapes = [a.shape for a in sums] + [(rows, taps), (gains, rows), (1, rows), (1, 2 * H)]
    return pl.pallas_call(
        functools.partial(results_kernel, count, taps, gains, heads_at),
        out_shape=[jax.ShapeDtypeStruct(shape, jnp.float32) for shape in shapes],
        in_specs=[VMEM] * (count + 1),
        out_specs=[ANY] * count + [VMEM] * 4,
        scratch_shapes=[dma(count)],
        compiler_params=pltpu.CompilerParams(vmem_limit_bytes=VMEM_LIMIT),
        name="results",
    )(*sums, small)


def edges(block, width):
    count = lax.axis_size("ctx")
    forward = [(i, i + 1) for i in range(count - 1)]
    backward = [(target, source) for source, target in forward]
    low = lax.ppermute(block[:, block.shape[1] - width :], "ctx", forward)
    high = lax.ppermute(block[:, :width], "ctx", backward)
    return low, high


def flat_rows(gathered):
    return [a.reshape(a.shape[0] * a.shape[1], a.shape[2]) for a in gathered]


def blocked(grad, shards):
    rows, cols = grad.shape
    return grad.astype(jnp.bfloat16).reshape(shards // 2, 2, rows // shards, cols)


def product(left, right):
    return jnp.dot(left, right, preferred_element_type=jnp.float32)


def product_left(left, right):
    return jnp.dot(left.T, right, preferred_element_type=jnp.float32)


def product_right(left, right):
    return jnp.dot(left, right.T, preferred_element_type=jnp.float32)


def swish(value):
    return value * jax.nn.sigmoid(value)


def swish_slope(value):
    sigma = jax.nn.sigmoid(value)
    return sigma * (1.0 + value * (1.0 - sigma))


def layer_norm(stream, gain):
    centred = stream - jnp.mean(stream, axis=-1, keepdims=True)
    inverse = lax.rsqrt(jnp.mean(centred * centred, axis=-1, keepdims=True) + EPS)
    unit = centred * inverse
    return ((unit * gain).astype(jnp.bfloat16), unit, inverse)


def norm_back(dnormed, unit, inverse, gain):
    scaled = dnormed * gain
    dstream = inverse * (
        scaled
        - jnp.mean(scaled, axis=-1, keepdims=True)
        - unit * jnp.mean(scaled * unit, axis=-1, keepdims=True)
    )
    return (dstream, jnp.sum(dnormed * unit, axis=0))


def per_device(
    tokens,
    lengths,
    cotangent,
    first_up,
    first_down,
    project_in,
    project_out,
    pointwise_in,
    depthwise,
    pointwise_out,
    second_up,
    second_down,
    gains,
    batch_shift,
    head_terms,
):
    micro_count, seqs, local, width = tokens.shape
    batch = micro_count * seqs
    rows = batch * local
    shards = lax.axis_size("fsdp")
    taps = depthwise.shape[1]
    tap_rows = -(-taps // 8) * 8
    gain_count = gains.shape[0]
    bf16 = jnp.bfloat16
    start = (lax.axis_index("ctx") * local).astype(jnp.int32).reshape(1)
    frame_pos = start[0] + lax.iota(jnp.int32, local)
    lengths_flat = lengths.reshape(batch)
    mask = (frame_pos[None, :] < lengths_flat[:, None]).astype(jnp.float32).reshape(rows, 1)
    mask_micro = mask.reshape(micro_count, seqs * local, 1)

    small = jnp.concatenate([depthwise, gains.T, batch_shift[:, None]], axis=1)
    small_cols = small.shape[1]
    small_width = 256
    small = jnp.pad(small, ((0, 0), (0, small_width - small_cols)))
    early = Gather(
        [first_up, small, first_down, project_in], "fsdp", "ctx", (True, False, True, False)
    )
    (gathered,) = exchange([early], 0)
    whole_first_up, whole_small, whole_first_down, whole_project_in = flat_rows(gathered)
    small_rows = whole_small[:, :small_cols].astype(jnp.float32).T
    tap_weights = jnp.pad(small_rows[:taps], ((0, tap_rows - taps), (0, 0)))
    gain_rows = small_rows[taps : taps + gain_count]
    shift_row = small_rows[taps + gain_count]

    stream_in = tokens.reshape(rows, width).astype(jnp.float32)
    normed_first, unit_first, inverse_first = layer_norm(stream_in, gain_rows[0])
    up_first = product(normed_first, whole_first_up)
    act_first = swish(up_first).astype(bf16)
    stream_first = stream_in + 0.5 * product(act_first, whole_first_down)
    normed_attend, unit_attend, inverse_attend = layer_norm(stream_first, gain_rows[1])
    triple = product(normed_attend, whole_project_in).astype(bf16)
    queries = triple[:, :width].reshape(batch, local, width)
    keyvals = Gather([triple[:, width:]], "ctx")
    later = Gather([project_out, pointwise_in, pointwise_out, second_up], "fsdp", "ctx")
    ((keyvals,), gathered) = exchange([keyvals, later], 1)
    whole_project_out, whole_pointwise_in, whole_pointwise_out, whole_second_up = flat_rows(gathered)
    keyvals = keyvals.reshape(keyvals.shape[0], batch, local, 2 * width)
    context = attend(start, lengths_flat, head_terms, queries, keyvals).reshape(rows, width)
    stream_attend = stream_first + product(context, whole_project_out)
    normed_conv, unit_conv, inverse_conv = layer_norm(stream_attend, gain_rows[2])
    expanded = product(normed_conv, whole_pointwise_in)
    linear = expanded[:, :width]
    gate_sigma = jax.nn.sigmoid(expanded[:, width:])
    gated_low = (linear * gate_sigma * mask).astype(bf16).reshape(batch, local, width)
    low, high = edges(gated_low, HALO)
    padded = jnp.concatenate([low, gated_low, high], axis=1)
    depth = depth_apply(padded, tap_weights, taps).reshape(micro_count, seqs * local, width)

    own_count = jnp.sum(mask_micro, axis=1)
    own_sum = jnp.sum(mask_micro * depth, axis=1)
    own_mean = own_sum / jnp.maximum(own_count, 1.0)
    own_centred = depth - own_mean[:, None, :]
    own_spread = jnp.sum(mask_micro * own_centred * own_centred, axis=1)
    moments = jnp.concatenate(
        [own_sum, own_spread, jnp.broadcast_to(own_count, own_sum.shape)], axis=0
    )
    moment_rows = -(-moments.shape[0] // 8) * 8
    moments = jnp.pad(moments, ((0, moment_rows - moments.shape[0]), (0, 0)))
    merging = Channels(moments, functools.partial(merge_moments, micro_count))
    last = Gather([second_down], "fsdp", "ctx", (True,))
    ((moments,), gathered) = exchange([merging, last], 2)
    (whole_second_down,) = flat_rows(gathered)
    count = moments[2 * micro_count : 3 * micro_count][:, None, :]
    bn_mean = moments[:micro_count][:, None, :] / count
    inverse_bn = lax.rsqrt(moments[micro_count : 2 * micro_count][:, None, :] / count + EPS)
    unit_bn = (depth - bn_mean) * inverse_bn
    shifted = unit_bn * gain_rows[5] + shift_row
    act_conv = swish(shifted).astype(bf16).reshape(rows, width)
    stream_conv = stream_attend + product(act_conv, whole_pointwise_out)
    normed_second, unit_second, inverse_second = layer_norm(stream_conv, gain_rows[3])
    up_second = product(normed_second, whole_second_up)
    act_second = swish(up_second).astype(bf16)
    stream_second = stream_conv + 0.5 * product(act_second, whole_second_down)
    out_low, unit_out, inverse_out = layer_norm(stream_second, gain_rows[4])
    output = out_low.reshape(tokens.shape)

    dout = cotangent.reshape(rows, width).astype(jnp.float32)
    dsecond_stream, gain_out = norm_back(dout, unit_out, inverse_out, gain_rows[4])
    dsecond_low = (0.5 * dsecond_stream).astype(bf16)
    dup_second = (product_right(dsecond_low, whole_second_down) * swish_slope(up_second)).astype(
        bf16
    )
    dtemp, gain_second = norm_back(
        product_right(dup_second, whole_second_up), unit_second, inverse_second, gain_rows[3]
    )
    grad_second_up = product_left(normed_second, dup_second)
    grad_second_down = product_left(act_second, dsecond_low)
    dconv_stream = dsecond_stream + dtemp
    dconv_low = dconv_stream.astype(bf16)
    dshift = product_right(dconv_low, whole_pointwise_out).reshape(depth.shape) * swish_slope(
        shifted
    )
    own_shift = jnp.sum(dshift, axis=1)
    own_cross = jnp.sum(dshift * unit_bn, axis=1)
    channel = jnp.concatenate([own_shift, own_cross], axis=0)
    channel_rows = -(-channel.shape[0] // 8) * 8
    channel = jnp.pad(channel, ((0, channel_rows - channel.shape[0]), (0, 0)))
    ((channel,),) = exchange([Channels(channel, merge_sums)], 3)
    sum_shift = channel[:micro_count][:, None, :]
    sum_cross = channel[micro_count : 2 * micro_count][:, None, :]
    ddepth = (
        inverse_bn
        * gain_rows[5]
        * (dshift - mask_micro * sum_shift / count - mask_micro * unit_bn * sum_cross / count)
    ).reshape(batch, local, width)
    dlow, dhigh = edges(ddepth.astype(bf16), HALO)
    dgated, tap_grads = depth_back(padded, dlow, dhigh, ddepth, tap_weights, taps)
    dgated = dgated.reshape(rows, width) * mask
    dexpanded = jnp.concatenate(
        [dgated * gate_sigma, dgated * linear * gate_sigma * (1.0 - gate_sigma)], axis=1
    ).astype(bf16)
    dtemp, gain_conv = norm_back(
        product_right(dexpanded, whole_pointwise_in), unit_conv, inverse_conv, gain_rows[2]
    )
    dattend_stream = dconv_stream + dtemp
    dattend_low = dattend_stream.astype(bf16)
    dcontext = product_right(dattend_low, whole_project_out).astype(bf16)
    dquery, dkeyvals, dheads = attend_back(
        start, lengths_flat, head_terms, queries, keyvals, dcontext.reshape(batch, local, width)
    )
    splits = dkeyvals.shape[0] // 2
    dkeyvals = dkeyvals.reshape(splits, 2, rows, 2 * width)
    conv_grads = [
        product_left(normed_conv, dexpanded),
        product_left(act_conv, dconv_low),
        product_left(context, dattend_low),
        grad_second_down,
        grad_second_up,
    ]
    ((dkeyvals,), conv_sums) = exchange(
        [
            Scatter([dkeyvals], "ctx", None, bf16),
            Scatter([blocked(g, shards) for g in conv_grads], "fsdp", "ctx", jnp.float32),
        ],
        4,
    )
    (
        grad_pointwise_in,
        grad_pointwise_out,
        grad_project_out,
        grad_second_down,
        grad_second_up,
    ) = conv_sums
    dtriple = jnp.concatenate([dquery.reshape(rows, width), dkeyvals], axis=1)
    dtemp, gain_attend = norm_back(
        product_right(dtriple, whole_project_in), unit_attend, inverse_attend, gain_rows[1]
    )
    dfirst_stream = dattend_stream + dtemp
    dfirst_low = (0.5 * dfirst_stream).astype(bf16)
    dup_first = (product_right(dfirst_low, whole_first_down) * swish_slope(up_first)).astype(bf16)
    dtemp, gain_first = norm_back(
        product_right(dup_first, whole_first_up), unit_first, inverse_first, gain_rows[0]
    )
    grad_tokens = (dfirst_stream + dtemp).astype(bf16).reshape(tokens.shape)

    small_grads = jnp.concatenate(
        [
            jnp.sum(tap_grads, axis=0)[:taps],
            jnp.stack([gain_first, gain_attend, gain_conv, gain_second, gain_out]),
            jnp.sum(own_cross, axis=0, keepdims=True),
            jnp.sum(own_shift, axis=0, keepdims=True),
        ],
        axis=0,
    ).T
    head_row = jnp.sum(dheads, axis=(0, 2)).reshape(1, 1, 2 * H)
    shard_rows = width // shards
    head_block = jnp.pad(
        jnp.broadcast_to(head_row, (shards, 1, 2 * H)),
        ((0, 0), (0, shard_rows - 1), (small_width // 2, small_width // 2 - 2 * H)),
    ).reshape(width, small_width)
    small_block = jnp.pad(small_grads, ((0, 0), (0, small_width - small_cols))) + head_block
    grads = [
        product_left(act_first, dfirst_low),
        product_left(normed_first, dup_first),
        product_left(normed_attend, dtriple),
        small_block,
    ]
    (sums,) = exchange(
        [Scatter([blocked(g, shards) for g in grads], "fsdp", "ctx", jnp.float32)], 5
    )
    grad_first_down, grad_first_up, grad_project_in, small_sum = sums
    (
        grad_first_up,
        grad_first_down,
        grad_project_in,
        grad_project_out,
        grad_pointwise_in,
        grad_pointwise_out,
        grad_second_up,
        grad_second_down,
        grad_depthwise,
        grad_gains,
        grad_shift,
        grad_heads,
    ) = results(
        [
            grad_first_up,
            grad_first_down,
            grad_project_in,
            grad_project_out,
            grad_pointwise_in,
            grad_pointwise_out,
            grad_second_up,
            grad_second_down,
        ],
        small_sum,
        taps,
        gain_count,
        small_width // 2,
    )
    return (
        output,
        grad_tokens,
        grad_first_up,
        grad_first_down,
        grad_project_in,
        grad_project_out,
        grad_pointwise_in,
        grad_depthwise,
        grad_pointwise_out,
        grad_second_up,
        grad_second_down,
        grad_gains,
        grad_shift.reshape(batch_shift.shape),
        grad_heads.reshape(head_terms.shape),
    )


def solution(mesh):
    in_specs = (
        P(None, "fsdp", "ctx", None),
        P(None, "fsdp"),
        P(None, "fsdp", "ctx", None),
        P("fsdp", None),
        P("fsdp", None),
        P("fsdp", None),
        P("fsdp", None),
        P("fsdp", None),
        P("fsdp", None),
        P("fsdp", None),
        P("fsdp", None),
        P("fsdp", None),
        P(None, "fsdp"),
        P("fsdp"),
        P(),
    )
    out_specs = (
        P(None, "fsdp", "ctx", None),
        P(None, "fsdp", "ctx", None),
        P("fsdp", None),
        P("fsdp", None),
        P("fsdp", None),
        P("fsdp", None),
        P("fsdp", None),
        P("fsdp", None),
        P("fsdp", None),
        P("fsdp", None),
        P("fsdp", None),
        P(None, "fsdp"),
        P("fsdp"),
        P(),
    )
    return jax.shard_map(
        per_device, mesh=mesh, in_specs=in_specs, out_specs=out_specs, check_vma=False
    )
```
